512 devices in a mesh: user: 32 (over x, y_lo, core), item: 16 (over y_hi, z).
Axes of the slice: x: 4, y: 8 (y_hi: 2, y_lo: 4; y = y_hi * 4 + y_lo), z: 8, core: 2. Of those that a mesh axis runs over, the one named last changes fastest.
Arguments:
- user_emb: bfloat16 [8192, 64], P('user'), may hold values from -300 to 300
- item_emb: bfloat16 [64, 262144], P(None, ('item', 'user')), may hold values from -1.5 to 1.5
- objective_weights: float32 [4], replicated, may hold values from 0.5 to 1.5
- objective_targets: float32 [4], replicated, may hold values from 0.2 to 0.6
- objective_duals: float32 [4], replicated, may hold values from -0.5 to 0.5
- capacity_duals: float32 [262144], P('item'), may hold values from 0 to 1
- capacity: float32 [262144], P('item'), may hold values from 0.5 to 2
Outputs:
- user_soft_value: float32 [8192], P('user')
- capacity_out: float32 [262144], P('item')
- objective_out: float32 [4], replicated
The draws below stay inside these ranges and needn't reach their ends.
All inputs are finite; a program needn't handle non-finite values.
Results may differ from the reference program's by a relative error of at most 0.0034.
Values may be sent and summed in bfloat16 or wider, within the bound.
A program may use at most 64 MiB of HBM per device.

```python
import math
import jax
import jax.numpy as jnp
from jax import lax

USER_DEV = 256
ITEMS = 262144
TOWERS = 4
EMBED = 16
ITERS = 2
FEAT = 64
USERS = 8192


def draw_user_emb(key, part):
    base_key = jax.random.fold_in(key, 11)
    offset_key = jax.random.fold_in(key, 14)
    values = jnp.clip(jax.random.normal(base_key, (USERS, FEAT), jnp.float32), -5.0, 5.0) * 0.75
    group_count = USERS // USER_DEV
    offsets = jnp.clip(jax.random.normal(offset_key, (group_count, FEAT), jnp.float32), -4.0, 4.0) * 0.65
    values = values + jnp.repeat(offsets, USER_DEV, axis=0)
    return values.astype(jnp.bfloat16)


def level_of(rng, shape, cuts, low, largest):
    def one(position, blocks):
        draws = jax.random.uniform(jax.random.fold_in(jax.random.fold_in(rng, 6), position), (blocks,), jnp.float32, low / len(cuts), largest / len(cuts))
        return jnp.repeat(jnp.exp(draws), shape[position] // blocks).reshape((-1,) + (1,) * (len(shape) - position - 1))

    factor_of = one(*cuts[0])
    for cut in cuts[1:]:
        factor_of = factor_of * one(*cut)
    return factor_of


def bell_draw(key, extent, spread, reach, split=(), held_as=jnp.bfloat16):
    drawn = spread * jax.random.normal(key, extent, jnp.float32)
    if split:
        drawn = drawn * level_of(key, extent, split, -0.22, 0.18)
    return jnp.clip(drawn, -reach, reach).astype(held_as)


def setup_inputs(seed: int = 0) -> dict:
    seeds = jax.random.split(jax.random.key(seed), 8)
    user_emb = draw_user_emb(jax.random.fold_in(seeds[7], 71), 0)
    item_emb = bell_draw(seeds[1], (FEAT, ITEMS), EMBED ** -0.5, 1.5, ((1, 512),))
    objective_weights = jnp.clip(jax.random.uniform(seeds[2], (TOWERS,), jnp.float32, 0.5, 1.5), 0.5, 1.5)
    objective_targets = jnp.clip(jax.random.uniform(seeds[3], (TOWERS,), jnp.float32, 0.2, 0.6), 0.2, 0.6)
    objective_duals = jnp.clip(jax.random.uniform(seeds[4], (TOWERS,), jnp.float32, -0.5, 0.5), -0.5, 0.5)
    capacity_duals = jnp.clip(1.0 * jax.random.uniform(seeds[5], (ITEMS,), jnp.float32) ** level_of(seeds[5], (ITEMS,), ((0, 16),), -0.2, 0.2), 0.0, 1.0)
    capacity = jnp.clip(jnp.exp(math.log(2.0) - 1.3862944 * jax.random.uniform(seeds[6], (ITEMS,), jnp.float32) ** level_of(seeds[6], (ITEMS,), ((0, 16),), -0.2, 0.2)), 0.5, 2.0)
    return dict(user_emb=user_emb, item_emb=item_emb, objective_weights=objective_weights, objective_targets=objective_targets, objective_duals=objective_duals, capacity_duals=capacity_duals, capacity=capacity)


softness_level = 2.0
dual_step = 0.5
target_step = 4.0


def reference(user_emb, item_emb, objective_weights, objective_targets, objective_duals, capacity_duals, capacity):
    block_cols = min(8192, ITEMS)
    block_count = ITEMS // block_cols
    item_blocks = item_emb.reshape(FEAT, block_count, block_cols).transpose(1, 0, 2)
    user_float = user_emb.astype(jnp.float32)
    tower_duals = objective_duals
    dual_now = capacity_duals
    user_soft_value = jnp.zeros((USERS,), jnp.float32)
    for iteration in range(ITERS):
        tower_coeff = objective_weights + tower_duals
        tempered_user_rows = (user_float * jnp.repeat(tower_coeff, EMBED)[None, :]).astype(jnp.bfloat16)
        dual_blocks = dual_now.reshape(block_count, block_cols)

        def stat_step(running, inputs):
            row_max_logit, row_exp_sum = running
            block_item_vectors, block_dual_prices = inputs
            user_item_logits = (jnp.dot(tempered_user_rows, block_item_vectors, preferred_element_type=jnp.float32) - block_dual_prices[None, :]) / softness_level
            new_max = jnp.maximum(row_max_logit, jnp.max(user_item_logits, axis=1))
            row_exp_sum = row_exp_sum * jnp.exp(row_max_logit - new_max) + jnp.sum(jnp.exp(user_item_logits - new_max[:, None]), axis=1)
            return (new_max, row_exp_sum), None

        start_state = (jnp.full((USERS,), -1e30, jnp.float32), jnp.zeros((USERS,), jnp.float32))
        (row_max_logit, row_exp_sum), unused = lax.scan(stat_step, start_state, (item_blocks, dual_blocks))
        user_soft_value = softness_level * (row_max_logit + jnp.log(row_exp_sum))

        def allocate_step(tower_sums, inputs):
            block_item_vectors, block_dual_prices = inputs
            user_item_logits = (jnp.dot(tempered_user_rows, block_item_vectors, preferred_element_type=jnp.float32) - block_dual_prices[None, :]) / softness_level
            exposure = jnp.exp(user_item_logits - row_max_logit[:, None]) / row_exp_sum[:, None]
            block_load = jnp.sum(exposure, axis=0)
            tower_sums = tower_sums + lax.dot_general(exposure.astype(jnp.bfloat16), block_item_vectors, (((1,), (1,)), ((), ())), preferred_element_type=jnp.float32)
            return tower_sums, block_load

        tower_sums, load_blocks = lax.scan(allocate_step, jnp.zeros((USERS, FEAT), jnp.float32), (item_blocks, dual_blocks))
        item_load = load_blocks.reshape(ITEMS)
        achieved = jnp.sum((user_float * tower_sums).reshape(USERS, TOWERS, EMBED), axis=(0, 2)) / USERS
        dual_now = jnp.maximum(0.0, dual_now + dual_step * (item_load * ITEMS / USERS - capacity))
        tower_duals = tower_duals + target_step * (objective_targets - achieved)
    return user_soft_value, dual_now, tower_duals
```

```python
import functools
from types import SimpleNamespace

import jax
import jax.numpy as jnp
from jax import lax
from jax.experimental import pallas as pl
from jax.experimental.pallas import tpu as pltpu
from jax.sharding import PartitionSpec as P

ITERS = 2
TAU = 2.0
DUAL_STEP = 0.5
TARGET_STEP = 4.0
MESH = pl.DeviceIdType.MESH

SLICE = SimpleNamespace(X=4, YL=4, C=2, YH=2, Z=8)

F32 = jnp.float32
BF16 = jnp.bfloat16
UD = 256
IB = 512
KD = 128


def kernel(
    g,
    user_ref, item_ref, ow_ref, ot_ref, od_ref, duals_ref, cap_ref,
    soft_out, cap_out, obj_out,
    upk, iaug, uaug, zbuf, ebuf, macc, sacc, tacc, wl, lam, capl,
    yms, yn, zms, zn, xload, xach, agbuf,
    gi_s, gi_r, gu_s, gu_r,
    yms_s, yms_r, yn_s, yn_r, zms_s, zms_r, zn_s, zn_r,
    xl_s, xl_r, xa_s, xa_r, ag_s, ag_r,
):
    X, YL, C, YH, Z = g.X, g.YL, g.C, g.YH, g.Z
    Y, XC = YL * YH, X * C
    NU = UD * YL
    NC = NU // 128
    users_total = UD * X * YL * C
    items_total = IB * X * YL * C * YH * Z
    ui = lax.axis_index("user")
    ii = lax.axis_index("item")
    c = ui % C
    yl = (ui // C) % YL
    x = ui // (C * YL)
    yh = ii // Z
    z = ii % Z
    y = yh * YL + yl
    xc = x * C + c

    def dev(x_, y_, c_, z_):
        return ((x_ * YL + y_ % YL) * C + c_, (y_ // YL) * Z + z_)

    ypeers = [dev(x, (y + d) % Y, c, z) for d in range(1, Y)]
    zpeers = [dev(x, y, c, (z + d) % Z) for d in range(1, Z)]
    xpeers = [
        dev((x + dx) % X, y, (c + dc) % C, z)
        for dx in range(X) for dc in range(C) if (dx, dc) != (0, 0)
    ]
    lpeers = [dev(x, yh * YL + (yl + d) % YL, c, z) for d in range(1, YL)]

    barrier = pltpu.get_barrier_semaphore()
    peers = ypeers + zpeers + xpeers
    for p in peers:
        pl.semaphore_signal(barrier, inc=1, device_id=p, device_id_type=MESH)

    up = jnp.concatenate(
        [user_ref[0:128, :].astype(F32), user_ref[128:256, :].astype(F32)], axis=1
    ).astype(BF16)
    upk[yl] = up
    iaug[xc, 0:64, :] = item_ref[...]
    for b in range(XC):
        iaug[b, 64:128, :] = jnp.zeros((64, IB), BF16)
    RX = 4 * C
    for xx in range(X):
        base = pl.multiple_of((xx * YL + yl) * RX, RX)
        lam[xx * RX:(xx + 1) * RX, :] = duals_ref[pl.ds(base, RX), :]
        capl[xx * RX:(xx + 1) * RX, :] = cap_ref[pl.ds(base, RX), :]

    pl.semaphore_wait(barrier, len(peers))

    def copies(src, dst, ss, rs, targets):
        out = [
            pltpu.make_async_remote_copy(
                src_ref=src, dst_ref=dst, send_sem=ss.at[k], recv_sem=rs.at[k],
                device_id=t, device_id_type=MESH,
            )
            for k, t in enumerate(targets)
        ]
        for q in out:
            q.start()
        return out

    pending = []
    gu = copies(upk.at[yl], upk.at[yl], gu_s, gu_r, lpeers)
    gi = copies(item_ref, iaug.at[xc, pl.ds(0, 64), :], gi_s, gi_r, xpeers)
    pending += gu + gi

    lane = lax.broadcasted_iota(jnp.int32, (1, 128), 1)
    tower = (lane % 64) // 16
    lane128 = lax.broadcasted_iota(jnp.int32, (128, 128), 1)
    sub16 = lax.broadcasted_iota(jnp.int32, (16, 128), 0)

    def by_tower(vals):
        out = jnp.zeros((1, 128), F32)
        for k in range(4):
            out = jnp.where(tower == k, vals[k], out)
        return out

    owv = by_tower([ow_ref[k] for k in range(4)])
    otv = by_tower([ot_ref[k] for k in range(4)])
    mu = by_tower([od_ref[k] for k in range(4)])

    def put_lambda():
        lv = lam[...]
        hi = lv.astype(BF16).astype(F32)
        r1 = lv - hi
        mid = r1.astype(BF16).astype(F32)
        lo = (r1 - mid).astype(BF16).astype(F32)
        for r in range(4 * XC):
            t = jnp.where(
                sub16 == 0, hi[r:r + 1, :],
                jnp.where(sub16 == 1, mid[r:r + 1, :],
                          jnp.where(sub16 == 2, lo[r:r + 1, :], 0.0)))
            iaug[r // 4, 64:80, (r % 4) * 128:(r % 4 + 1) * 128] = t.astype(BF16)

    put_lambda()
    for q in gu:
        q.wait_recv()

    def put_users(muv):
        coef = owv + muv

        def body(b, carry):
            pk = upk[b].astype(F32)
            sc = (pk * coef).astype(BF16).astype(F32) * (1.0 / TAU)
            for h in range(2):
                t = sc if h == 0 else pltpu.roll(sc, 64, 1)
                t = jnp.where(lane128 < 64, t, jnp.where(lane128 < 67, -1.0 / TAU, 0.0))
                uaug[pl.ds(pl.multiple_of(b * 256 + h * 128, 128), 128), :] = t.astype(BF16)
            return carry

        lax.fori_loop(0, YL, body, 0)

    put_users(mu)
    for q in gi:
        q.wait_recv()

    NUB = NU // 256

    for it in range(ITERS):
        macc[...] = jnp.full((NU, 128), -3.0e38, F32)

        def pass1(t, carry):
            b, ub = t // NUB, t % NUB
            rows = pl.ds(pl.multiple_of(ub * 256, 256), 256)
            zt = jnp.dot(uaug[rows, :], iaug[b], preferred_element_type=F32)
            zbuf[b, rows, :] = zt
            m = jnp.maximum(jnp.maximum(zt[:, 0:128], zt[:, 128:256]),
                            jnp.maximum(zt[:, 256:384], zt[:, 384:512]))
            macc[rows, :] = jnp.maximum(macc[rows, :], m)
            return carry

        lax.fori_loop(0, XC * NUB, pass1, 0)
        for q in range(NC):
            rows = slice(q * 128, (q + 1) * 128)
            m = jnp.max(macc[rows, :], axis=1, keepdims=True)
            macc[rows, :] = jnp.broadcast_to(m, (128, 128))
        sacc[...] = jnp.zeros((NU, 128), F32)
        tacc[...] = jnp.zeros((NU, 128), F32)

        def pass2(t, carry):
            b, ub = t // NUB, t % NUB
            rows = pl.ds(pl.multiple_of(ub * 256, 256), 256)
            mb = macc[rows, :]
            parts = [jnp.exp(zbuf[b, rows, k * 128:(k + 1) * 128] - mb) for k in range(4)]
            sacc[rows, :] += (parts[0] + parts[1]) + (parts[2] + parts[3])
            e16 = jnp.concatenate(parts, axis=1).astype(BF16)
            ebuf[b, rows, :] = e16
            tacc[rows, :] += lax.dot_general(
                e16, iaug[b], (((1,), (1,)), ((), ())), preferred_element_type=F32)
            return carry

        lax.fori_loop(0, XC * NUB, pass2, 0)

        def stats(q, carry):
            rows = pl.ds(pl.multiple_of(q * 128, 128), 128)
            pk = upk[q // 2].astype(F32)
            uf = jnp.where(q % 2 == 0, pk, pltpu.roll(pk, 64, 1))
            p = jnp.where(lane128 < 64, uf * tacc[rows, :], macc[rows, :])
            pt = p.T
            st = sacc[rows, :].T
            one = pl.ds(q, 1)
            yms[it, y, 0, one, :] = pt[64:65, :]
            yms[it, y, 1, one, :] = jnp.sum(st, axis=0, keepdims=True)
            for k in range(4):
                yn[it, y, k, one, :] = jnp.sum(pt[16 * k:16 * k + 16, :], axis=0, keepdims=True)
            return carry

        lax.fori_loop(0, NC, stats, 0)

        cy_ms = copies(yms.at[it, y], yms.at[it, y], yms_s.at[it], yms_r.at[it], ypeers)
        cy_n = copies(yn.at[it, y], yn.at[it, y], yn_s.at[it], yn_r.at[it], ypeers)
        m_loc = yms[it, y, 0]
        for q in cy_ms:
            q.wait_recv()
        ms = yms[it]
        my = jnp.max(ms[:, 0], axis=0)
        fy = jnp.exp(ms[:, 0] - my[None])
        zms[it, z, 0] = my
        zms[it, z, 1] = jnp.sum(ms[:, 1] * fy, axis=0)
        cz_ms = copies(zms.at[it, z], zms.at[it, z], zms_s.at[it], zms_r.at[it], zpeers)
        for q in cy_n:
            q.wait_recv()
        nv = yn[it]
        for k in range(4):
            zn[it, z, k] = jnp.sum(nv[:, k] * fy, axis=0)
        cz_n = copies(zn.at[it, z], zn.at[it, z], zn_s.at[it], zn_r.at[it], zpeers)
        for q in cz_ms:
            q.wait_recv()
        ms = zms[it]
        mg = jnp.max(ms[:, 0], axis=0)
        fz = jnp.exp(ms[:, 0] - mg[None])
        sg = jnp.sum(ms[:, 1] * fz, axis=0)
        inv = 1.0 / sg
        w = jnp.exp(m_loc - mg) * inv
        if it == ITERS - 1:
            macc[0:NC, :] = TAU * (mg + jnp.log(sg))
            soft_out[...] = macc[pl.ds(yl * 2, 2), :]
        whi = w.astype(BF16).astype(F32)
        r1 = w - whi
        wmid = r1.astype(BF16).astype(F32)
        wlo = (r1 - wmid).astype(BF16).astype(F32)
        for q in range(NC):
            t = jnp.where(
                sub16 == 0, whi[q:q + 1, :],
                jnp.where(sub16 == 1, wmid[q:q + 1, :],
                          jnp.where(sub16 == 2, wlo[q:q + 1, :], 0.0)))
            wl[:, q * 128:(q + 1) * 128] = t.astype(BF16)
        for b in range(XC):
            acc = jnp.dot(wl[...], ebuf[b], preferred_element_type=F32)
            row = acc[0:1, :] + acc[1:2, :] + acc[2:3, :]
            for k in range(4):
                xload[it, xc, 4 * b + k:4 * b + k + 1, :] = row[:, k * 128:(k + 1) * 128]
        cx_l = copies(xload.at[it, xc], xload.at[it, xc], xl_s.at[it], xl_r.at[it], xpeers)
        for q in cz_n:
            q.wait_recv()
        nv = zn[it]
        xach[it, xc] = jnp.zeros((8, 128), F32)
        for k in range(4):
            t = jnp.sum(nv[:, k] * fz, axis=0) * inv
            xach[it, xc, k:k + 1, :] = jnp.sum(t, axis=0, keepdims=True)
        cx_a = copies(xach.at[it, xc], xach.at[it, xc], xa_s.at[it], xa_r.at[it], xpeers)
        for q in cx_a:
            q.wait_recv()
        ach = jnp.sum(jnp.sum(xach[it], axis=0), axis=1, keepdims=True) / users_total
        achv = by_tower([ach[k:k + 1, :] for k in range(4)])
        mu = mu + TARGET_STEP * (otv - achv)
        if it < ITERS - 1:
            put_users(mu)
        for q in cx_l:
            q.wait_recv()
        load = jnp.sum(xload[it], axis=0)
        lam[...] = jnp.maximum(
            0.0, lam[...] + DUAL_STEP * (load * (items_total / users_total) - capl[...]))
        if it < ITERS - 1:
            put_lambda()
        pending += cy_ms + cy_n + cz_ms + cz_n + cx_l + cx_a

    agbuf[yl] = lam[...]
    if YL > 1:
        ca = copies(agbuf.at[yl], agbuf.at[yl], ag_s, ag_r, lpeers)
        for q in ca:
            q.wait_recv()
        pending += ca
    for l in range(YL):
        for xx in range(X):
            cap_out[(xx * YL + l) * RX:(xx * YL + l + 1) * RX, :] = agbuf[l, xx * RX:(xx + 1) * RX, :]
    for k in range(4):
        obj_out[k] = jnp.max(jnp.where(lane == 16 * k, mu, -3.0e38))
    for q in pending:
        q.wait_send()


def per_device(g, user_emb, item_emb, ow, ot, od, duals, cap):
    X, YL, C, YH, Z = g.X, g.YL, g.C, g.YH, g.Z
    Y, XC, NU = YL * YH, X * C, UD * YL
    NC = NU // 128
    rows = IB * X * YL * C // 128
    vm = pl.BlockSpec(memory_space=pltpu.VMEM)
    sm = pl.BlockSpec(memory_space=pltpu.SMEM)
    dma = pltpu.SemaphoreType.DMA
    V = pltpu.VMEM
    nl = max(YL - 1, 1)
    soft, capo, obj = pl.pallas_call(
        functools.partial(kernel, g),
        out_shape=(
            jax.ShapeDtypeStruct((UD // 128, 128), F32),
            jax.ShapeDtypeStruct((rows, 128), F32),
            jax.ShapeDtypeStruct((4,), F32),
        ),
        in_specs=[vm, vm, sm, sm, sm, vm, vm],
        out_specs=(vm, vm, sm),
        scratch_shapes=[
            V((YL, 128, 128), BF16),
            V((XC, KD, IB), BF16),
            V((NU, KD), BF16),
            V((XC, NU, IB), F32),
            V((XC, NU, IB), BF16),
            V((NU, 128), F32),
            V((NU, 128), F32),
            V((NU, 128), F32),
            V((16, NU), BF16),
            V((4 * XC, 128), F32),
            V((4 * XC, 128), F32),
            V((ITERS, Y, 2, NC, 128), F32),
            V((ITERS, Y, 4, NC, 128), F32),
            V((ITERS, Z, 2, NC, 128), F32),
            V((ITERS, Z, 4, NC, 128), F32),
            V((ITERS, XC, 4 * XC, 128), F32),
            V((ITERS, XC, 8, 128), F32),
            V((YL, 4 * XC, 128), F32),
            dma((XC - 1,)), dma((XC - 1,)), dma((nl,)), dma((nl,)),
            dma((ITERS, Y - 1)), dma((ITERS, Y - 1)), dma((ITERS, Y - 1)), dma((ITERS, Y - 1)),
            dma((ITERS, Z - 1)), dma((ITERS, Z - 1)), dma((ITERS, Z - 1)), dma((ITERS, Z - 1)),
            dma((ITERS, XC - 1)), dma((ITERS, XC - 1)), dma((ITERS, XC - 1)), dma((ITERS, XC - 1)),
            dma((nl,)), dma((nl,)),
        ],
        compiler_params=pltpu.CompilerParams(
            collective_id=0, has_side_effects=True, vmem_limit_bytes=60 * 1024 * 1024),
        name="dual_ascent",
    )(user_emb, item_emb, ow, ot, od, duals.reshape(rows, 128), cap.reshape(rows, 128))
    return soft.reshape(UD), capo.reshape(rows * 128), obj


def solution(mesh, g=SLICE):
    in_specs = (P("user", None), P(None, ("item", "user")), P(), P(), P(), P("item"), P("item"))
    out_specs = (P("user"), P("item"), P())
    return jax.shard_map(
        functools.partial(per_device, g), mesh=mesh, in_specs=in_specs, out_specs=out_specs,
        check_vma=False,
    )
```

```python
import functools
from types import SimpleNamespace

import jax
import jax.numpy as jnp
from jax import lax
from jax.experimental import pallas as pl
from jax.experimental.pallas import tpu as pltpu
from jax.sharding import PartitionSpec as P

ITERS = 2
TAU = 2.0
DUAL_STEP = 0.5
TARGET_STEP = 4.0
MESH = pl.DeviceIdType.MESH

SLICE = SimpleNamespace(X=4, YL=4, C=2, YH=2, Z=8)

F32 = jnp.float32
BF16 = jnp.bfloat16
UD = 256
IB = 512
KD = 128


def kernel(
    g,
    user_hbm, item_hbm, duals_hbm, cap_hbm, ow_ref, ot_ref, od_ref,
    soft_out, cap_out, obj_out,
    ut, uraw, iaug, uaug, zbuf, ebuf, macc, tacc, st, wl, lam, capl,
    yll, yn, zll, zn, xload, xach, agbuf,
    in_s, gi_s, gi_r, gu_s, gu_r,
    yl_s, yl_r, yn_s, yn_r, zl_s, zl_r, zn_s, zn_r,
    xl_s, xl_r, xa_s, xa_r, ag_s, ag_r,
):
    X, YL, C, YH, Z = g.X, g.YL, g.C, g.YH, g.Z
    Y, XC = YL * YH, X * C
    NU = UD * YL
    NC = NU // 128
    users_total = UD * X * YL * C
    items_total = IB * X * YL * C * YH * Z
    ui = lax.axis_index("user")
    ii = lax.axis_index("item")
    c = ui % C
    yl = (ui // C) % YL
    x = ui // (C * YL)
    yh = ii // Z
    z = ii % Z
    y = yh * YL + yl
    xc = x * C + c

    def dev(x_, y_, c_, z_):
        return ((x_ * YL + y_ % YL) * C + c_, (y_ // YL) * Z + z_)

    def far_first(n):
        return sorted(range(1, n), key=lambda d: -min(d, n - d))

    near = far_first(X)[::-1]
    ypeers = [dev(x, (y + d) % Y, c, z) for d in far_first(Y)]
    zpeers = [dev(x, y, c, (z + d) % Z) for d in far_first(Z)]
    xpeers = [
        dev((x + dx) % X, y, (c + dc) % C, z)
        for dx in far_first(X) + [0] for dc in range(C) if (dx, dc) != (0, 0)
    ]
    lpeers = [dev(x, yh * YL + (yl + d) % YL, c, z) for d in range(1, YL)]

    barrier = pltpu.get_barrier_semaphore()
    peers = ypeers + zpeers + xpeers
    for p in peers:
        pl.semaphore_signal(barrier, inc=1, device_id=p, device_id_type=MESH)

    own_items = iaug.at[xc, pl.ds(0, 64), :]
    local = [
        pltpu.make_async_copy(user_hbm, ut.at[yl], in_s.at[0]),
        pltpu.make_async_copy(item_hbm, own_items, in_s.at[1]),
    ]
    RX = 4 * C
    for xx in range(X):
        rows = pl.ds(pl.multiple_of((xx * YL + yl) * RX, RX), RX)
        mine = pl.ds(xx * RX, RX)
        local.append(pltpu.make_async_copy(duals_hbm.at[rows], lam.at[mine], in_s.at[2 + 2 * xx]))
        local.append(pltpu.make_async_copy(cap_hbm.at[rows], capl.at[mine], in_s.at[3 + 2 * xx]))
    for q in local:
        q.start()
    for b in range(XC):
        iaug[b, 64:128, :] = jnp.zeros((64, IB), BF16)
    for q in local:
        q.wait()

    def send(src, dst, ss, rs, target):
        q = pltpu.make_async_remote_copy(
            src_ref=src, dst_ref=dst, send_sem=ss, recv_sem=rs,
            device_id=target, device_id_type=MESH)
        q.start()
        return q

    def copies(src, dst, ss, rs, targets):
        return [send(src, dst, ss.at[k], rs.at[k], t) for k, t in enumerate(targets)]

    lane = lax.broadcasted_iota(jnp.int32, (1, 128), 1)
    tower = lane // 16
    lane128 = lax.broadcasted_iota(jnp.int32, (128, 128), 1)
    sub16 = lax.broadcasted_iota(jnp.int32, (16, 128), 0)
    sub64 = lax.broadcasted_iota(jnp.int32, (64, 128), 0)

    def by_tower(vals, rest):
        out = jnp.full((1, 128), rest, F32)
        for k in range(4):
            out = jnp.where(tower == k, vals[k], out)
        return out

    owv = by_tower([ow_ref[k] for k in range(4)], 1.0)
    otv = by_tower([ot_ref[k] for k in range(4)], 0.0)
    mu = by_tower([od_ref[k] for k in range(4)], 0.0)

    def put_lambda():
        lv = lam[...]
        hi = lv.astype(BF16).astype(F32)
        r1 = lv - hi
        mid = r1.astype(BF16).astype(F32)
        lo = (r1 - mid).astype(BF16).astype(F32)
        for r in range(4 * XC):
            t = jnp.where(
                sub16 == 0, hi[r:r + 1, :],
                jnp.where(sub16 == 1, mid[r:r + 1, :],
                          jnp.where(sub16 == 2, lo[r:r + 1, :],
                                    jnp.where(sub16 == 3, 1.0, 0.0))))
            iaug[r // 4, 64:80, (r % 4) * 128:(r % 4 + 1) * 128] = t.astype(BF16)

    put_lambda()
    minus = jnp.where(sub64 < 3, -1.0, 0.0)

    def put_raw(b):
        for h in range(2):
            blk = ut[b, :, h * 128:(h + 1) * 128].astype(F32)
            rows = pl.ds(pl.multiple_of(b * 256 + h * 128, 128), 128)
            uraw[rows, :] = jnp.concatenate([blk, minus], axis=0).T.astype(BF16)

    put_raw(yl)
    pl.semaphore_wait(barrier, len(peers))

    pending = []
    gu = copies(ut.at[yl], ut.at[yl], gu_s, gu_r, lpeers)
    gi = [
        send(own_items, own_items, gi_s.at[k], gi_r.at[k], dev((x + d) % X, y, c, z))
        for k, d in enumerate(near)
    ]
    blocks = [(xc, None)]
    if C > 1:
        half = X - 1
        other = dev(x, y, 1 - c, z)
        blocks.append((x * C + 1 - c, send(
            own_items, own_items, gi_s.at[half], gi_r.at[half], other)))
        pending.append(blocks[-1][1])

    def relay(k):
        gi[k].wait_recv()
        src = (x + X - near[k]) % X
        blocks.append((src * C + c, None))
        if C > 1:
            ref = iaug.at[src * C + c, pl.ds(0, 64), :]
            q = send(ref, ref, gi_s.at[X + k], gi_r.at[X + k], other)
            pending.append(q)
            blocks.append((src * C + 1 - c, q))

    def put_users(muv):
        coef = owv + muv
        coef = jnp.where(lane < 64, coef, 1.0)
        for r in range(0, NU, 128):
            rows = slice(r, r + 128)
            sc = (uraw[rows, :].astype(F32) * coef).astype(BF16).astype(F32) * (1.0 / TAU)
            uaug[rows, :] = sc.astype(BF16)

    def logits(b, first):
        zt = jnp.dot(uaug[...], iaug[b], preferred_element_type=F32)
        zbuf[b] = zt
        m = jnp.maximum(jnp.maximum(zt[:, 0:128], zt[:, 128:256]),
                        jnp.maximum(zt[:, 256:384], zt[:, 384:512]))
        macc[...] = m if first else jnp.maximum(macc[...], m)

    def pass1_step(b, carry):
        logits(b, False)
        return carry

    def pass2_step(b, carry):
        mb = macc[...]
        parts = [jnp.exp(zbuf[b, :, k * 128:(k + 1) * 128] - mb) for k in range(4)]
        e16 = jnp.concatenate(parts, axis=1).astype(BF16)
        ebuf[b] = e16
        tacc[...] += lax.dot_general(
            e16, iaug[b], (((1,), (1,)), ((), ())), preferred_element_type=F32)
        return carry

    def lse(v):
        top = jnp.max(v, axis=0)
        return top + jnp.log(jnp.sum(jnp.exp(v - top[None]), axis=0))

    for it in range(ITERS):
        if it == 0:
            for k in range(min(2, len(near))):
                relay(k)
            for q in gu:
                q.wait_recv()
            for d in range(1, YL):
                put_raw((yl + d) % YL)
            put_users(mu)
            for k in range(XC):
                if k >= 2 and len(blocks) < XC:
                    relay(len(near) - 1)
                b, q = blocks[k]
                if q is not None:
                    q.wait_recv()
                logits(b, k == 0)
            pending += gu + gi
        else:
            logits(0, True)
            lax.fori_loop(1, XC, pass1_step, 0, unroll=True)
        for q in range(NC):
            rows = slice(q * 128, (q + 1) * 128)
            m = jnp.max(macc[rows, :], axis=1, keepdims=True)
            macc[rows, :] = jnp.broadcast_to(m, (128, 128))
        tacc[...] = jnp.zeros((NU, 128), F32)

        lax.fori_loop(0, XC, pass2_step, 0, unroll=2)

        for q in range(NC):
            rows = slice(q * 128, (q + 1) * 128)
            pt = jnp.where(lane128 == 64, macc[rows, :], tacc[rows, :]).T
            uf = ut[q // 2, :, (q % 2) * 128:(q % 2 + 1) * 128].astype(F32)
            prod = uf * pt[0:64, :]
            st[0, q:q + 1, :] = pt[64:65, :]
            st[1, q:q + 1, :] = pt[67:68, :]
            for k in range(4):
                st[2 + k, q:q + 1, :] = jnp.sum(prod[16 * k:16 * k + 16, :], axis=0, keepdims=True)

        m_loc = st[0]
        s_loc = st[1]
        yll[it, y] = m_loc + jnp.log(s_loc)
        cy_l = copies(yll.at[it, y], yll.at[it, y], yl_s.at[it], yl_r.at[it], ypeers)
        inv = 1.0 / s_loc
        for k in range(4):
            yn[it, y, k] = st[2 + k] * inv
        cy_n = copies(yn.at[it, y], yn.at[it, y], yn_s.at[it], yn_r.at[it], ypeers)
        for q in cy_l:
            q.wait_recv()
        lv = yll[it]
        ly = lse(lv)
        zll[it, z] = ly
        cz_l = copies(zll.at[it, z], zll.at[it, z], zl_s.at[it], zl_r.at[it], zpeers)
        fy = jnp.exp(lv - ly[None])
        for q in cy_n:
            q.wait_recv()
        nv = yn[it]
        for k in range(4):
            zn[it, z, k] = jnp.sum(nv[:, k] * fy, axis=0)
        cz_n = copies(zn.at[it, z], zn.at[it, z], zn_s.at[it], zn_r.at[it], zpeers)
        for q in cz_l:
            q.wait_recv()
        lv = zll[it]
        lg = lse(lv)
        w = jnp.exp(m_loc - lg)
        if it == ITERS - 1:
            macc[0:NC, :] = TAU * lg
            soft_out[...] = macc[pl.ds(yl * 2, 2), :]
        whi = w.astype(BF16).astype(F32)
        r1 = w - whi
        wmid = r1.astype(BF16).astype(F32)
        wlo = (r1 - wmid).astype(BF16).astype(F32)
        for q in range(NC):
            t = jnp.where(
                sub16 == 0, whi[q:q + 1, :],
                jnp.where(sub16 == 1, wmid[q:q + 1, :],
                          jnp.where(sub16 == 2, wlo[q:q + 1, :], 0.0)))
            wl[:, q * 128:(q + 1) * 128] = t.astype(BF16)
        for b in range(XC):
            acc = jnp.dot(wl[...], ebuf[b], preferred_element_type=F32)
            row = acc[0:1, :] + acc[1:2, :] + acc[2:3, :]
            for k in range(4):
                xload[it, xc, 4 * b + k:4 * b + k + 1, :] = row[:, k * 128:(k + 1) * 128]
        cx_l = copies(xload.at[it, xc], xload.at[it, xc], xl_s.at[it], xl_r.at[it], xpeers)
        fz = jnp.exp(lv - lg[None])
        for q in cz_n:
            q.wait_recv()
        nv = zn[it]
        xach[it, xc] = jnp.zeros((8, 128), F32)
        for k in range(4):
            t = jnp.sum(nv[:, k] * fz, axis=0)
            xach[it, xc, k:k + 1, :] = jnp.sum(t, axis=0, keepdims=True)
        cx_a = copies(xach.at[it, xc], xach.at[it, xc], xa_s.at[it], xa_r.at[it], xpeers)
        for q in cx_l:
            q.wait_recv()
        load = jnp.sum(xload[it], axis=0)
        lam[...] = jnp.maximum(
            0.0, lam[...] + DUAL_STEP * (load * (items_total / users_total) - capl[...]))
        if it < ITERS - 1:
            put_lambda()
        else:
            agbuf[yl] = lam[...]
            ca = copies(agbuf.at[yl], agbuf.at[yl], ag_s, ag_r, lpeers)
        for q in cx_a:
            q.wait_recv()
        ach = jnp.sum(jnp.sum(xach[it], axis=0), axis=1, keepdims=True) / users_total
        achv = by_tower([ach[k:k + 1, :] for k in range(4)], 0.0)
        mu = mu + TARGET_STEP * (otv - achv)
        if it < ITERS - 1:
            put_users(mu)
        pending += cy_l + cy_n + cz_l + cz_n + cx_l + cx_a

    for k in range(4):
        obj_out[k] = jnp.max(jnp.where(lane == 16 * k, mu, -3.0e38))
    for q in ca:
        q.wait_recv()
    for l in range(YL):
        for xx in range(X):
            cap_out[(xx * YL + l) * RX:(xx * YL + l + 1) * RX, :] = agbuf[l, xx * RX:(xx + 1) * RX, :]
    for q in pending + ca:
        q.wait_send()


def per_device(g, user_emb, item_emb, ow, ot, od, duals, cap):
    X, YL, C, YH, Z = g.X, g.YL, g.C, g.YH, g.Z
    Y, XC, NU = YL * YH, X * C, UD * YL
    NC = NU // 128
    rows = IB * X * YL * C // 128
    vm = pl.BlockSpec(memory_space=pltpu.VMEM)
    sm = pl.BlockSpec(memory_space=pltpu.SMEM)
    hbm = pl.BlockSpec(memory_space=pl.ANY)
    dma = pltpu.SemaphoreType.DMA
    V = pltpu.VMEM
    nl = max(YL - 1, 1)
    soft, capo, obj = pl.pallas_call(
        functools.partial(kernel, g),
        out_shape=(
            jax.ShapeDtypeStruct((UD // 128, 128), F32),
            jax.ShapeDtypeStruct((rows, 128), F32),
            jax.ShapeDtypeStruct((4,), F32),
        ),
        in_specs=[hbm, hbm, hbm, hbm, sm, sm, sm],
        out_specs=(vm, vm, sm),
        scratch_shapes=[
            V((YL, 64, UD), BF16),
            V((NU, KD), BF16),
            V((XC, KD, IB), BF16),
            V((NU, KD), BF16),
            V((XC, NU, IB), F32),
            V((XC, NU, IB), BF16),
            V((NU, 128), F32),
            V((NU, 128), F32),
            V((6, NC, 128), F32),
            V((16, NU), BF16),
            V((4 * XC, 128), F32),
            V((4 * XC, 128), F32),
            V((ITERS, Y, NC, 128), F32),
            V((ITERS, Y, 4, NC, 128), F32),
            V((ITERS, Z, NC, 128), F32),
            V((ITERS, Z, 4, NC, 128), F32),
            V((ITERS, XC, 4 * XC, 128), F32),
            V((ITERS, XC, 8, 128), F32),
            V((YL, 4 * XC, 128), F32),
            dma((2 + 2 * X,)),
            dma((2 * X,)), dma((2 * X,)), dma((nl,)), dma((nl,)),
            dma((ITERS, Y - 1)), dma((ITERS, Y - 1)), dma((ITERS, Y - 1)), dma((ITERS, Y - 1)),
            dma((ITERS, Z - 1)), dma((ITERS, Z - 1)), dma((ITERS, Z - 1)), dma((ITERS, Z - 1)),
            dma((ITERS, XC - 1)), dma((ITERS, XC - 1)), dma((ITERS, XC - 1)), dma((ITERS, XC - 1)),
            dma((nl,)), dma((nl,)),
        ],
        compiler_params=pltpu.CompilerParams(
            collective_id=0, has_side_effects=True, vmem_limit_bytes=60 * 1024 * 1024),
        name="dual_ascent",
    )(user_emb.T, item_emb, duals.reshape(rows, 128), cap.reshape(rows, 128), ow, ot, od)
    return soft.reshape(UD), capo.reshape(rows * 128), obj


def solution(mesh, g=SLICE):
    in_specs = (P("user", None), P(None, ("item", "user")), P(), P(), P(), P("item"), P("item"))
    out_specs = (P("user"), P("item"), P())
    return jax.shard_map(
        functools.partial(per_device, g), mesh=mesh, in_specs=in_specs, out_specs=out_specs,
        check_vma=False,
    )
```

```python
import functools
from types import SimpleNamespace

import jax
import jax.numpy as jnp
from jax import lax
from jax.experimental import pallas as pl
from jax.experimental.pallas import tpu as pltpu
from jax.sharding import PartitionSpec as P

ITERS = 2
TAU = 2.0
DUAL_STEP = 0.5
TARGET_STEP = 4.0
MESH = pl.DeviceIdType.MESH

SLICE = SimpleNamespace(X=4, YL=4, C=2, YH=2, Z=8)

F32 = jnp.float32
BF16 = jnp.bfloat16
UD = 256
IB = 512
KD = 128


def kernel(
    g,
    user_hbm, item_hbm, duals_hbm, cap_hbm, ow_hbm, ot_hbm, od_hbm,
    out,
    ow_ref, ot_ref, od_ref,
    ut, uraw, iaug, uaug, zbuf, ebuf, macc, sacc, tacc, st, wl, lam, capl,
    yll, yn, zll, zn, xload, xach, agbuf,
    in_s, gi_s, gi_r, gu_s, gu_r,
    yl_s, yl_r, yn_s, yn_r, zl_s, zl_r, zn_s, zn_r,
    xl_s, xl_r, xa_s, xa_r, ag_s, ag_r,
):
    X, YL, C, YH, Z = g.X, g.YL, g.C, g.YH, g.Z
    Y, XC = YL * YH, X * C
    NU = UD * YL
    NC = NU // 128
    users_total = UD * X * YL * C
    items_total = IB * X * YL * C * YH * Z
    ui = lax.axis_index("user")
    ii = lax.axis_index("item")
    c = ui % C
    yl = (ui // C) % YL
    x = ui // (C * YL)
    yh = ii // Z
    z = ii % Z
    y = yh * YL + yl
    xc = x * C + c

    def dev(x_, y_, c_, z_):
        return ((x_ * YL + y_ % YL) * C + c_, (y_ // YL) * Z + z_)

    def far_first(n):
        return sorted(range(1, n), key=lambda d: -min(d, n - d))

    ypeers = [dev(x, (y + d) % Y, c, z) for d in far_first(Y)]
    zpeers = [dev(x, y, c, (z + d) % Z) for d in far_first(Z)]
    xpeers = [
        dev((x + dx) % X, y, (c + dc) % C, z)
        for dx in far_first(X) + [0] for dc in range(C) if (dx, dc) != (0, 0)
    ]
    lpeers = [dev(x, yh * YL + (yl + d) % YL, c, z) for d in range(1, YL)]

    barrier = pltpu.get_barrier_semaphore()
    peers = ypeers + zpeers + xpeers
    for p in peers:
        pl.semaphore_signal(barrier, inc=1, device_id=p, device_id_type=MESH)

    own_items = iaug.at[xc, pl.ds(0, 64), :]
    local = [
        pltpu.make_async_copy(user_hbm, ut.at[yl], in_s.at[0]),
        pltpu.make_async_copy(item_hbm, own_items, in_s.at[1]),
        pltpu.make_async_copy(ow_hbm, ow_ref, in_s.at[2]),
        pltpu.make_async_copy(ot_hbm, ot_ref, in_s.at[3]),
        pltpu.make_async_copy(od_hbm, od_ref, in_s.at[4]),
    ]
    RX = 4 * C
    rows_out = RX * X * YL
    for xx in range(X):
        rows = pl.ds(pl.multiple_of((xx * YL + yl) * RX, RX), RX)
        mine = pl.ds(xx * RX, RX)
        local.append(pltpu.make_async_copy(duals_hbm.at[rows], lam.at[mine], in_s.at[5 + 2 * xx]))
        local.append(pltpu.make_async_copy(cap_hbm.at[rows], capl.at[mine], in_s.at[6 + 2 * xx]))
    for q in local:
        q.start()
    for b in range(XC):
        iaug[b, 64:128, :] = jnp.zeros((64, IB), BF16)
    for q in local:
        q.wait()

    def send(src, dst, ss, rs, target):
        q = pltpu.make_async_remote_copy(
            src_ref=src, dst_ref=dst, send_sem=ss, recv_sem=rs,
            device_id=target, device_id_type=MESH)
        q.start()
        return q

    def copies(src, dst, ss, rs, targets):
        return [send(src, dst, ss.at[k], rs.at[k], t) for k, t in enumerate(targets)]

    lane = lax.broadcasted_iota(jnp.int32, (1, 128), 1)
    tower = lane // 16
    lane128 = lax.broadcasted_iota(jnp.int32, (128, 128), 1)
    sub16 = lax.broadcasted_iota(jnp.int32, (16, 128), 0)
    sub64 = lax.broadcasted_iota(jnp.int32, (64, 128), 0)

    def by_tower(vals, rest):
        out = jnp.full((1, 128), rest, F32)
        for k in range(4):
            out = jnp.where(tower == k, vals[k], out)
        return out

    owv = by_tower([ow_ref[k] for k in range(4)], 1.0)
    otv = by_tower([ot_ref[k] for k in range(4)], 0.0)
    mu = by_tower([od_ref[k] for k in range(4)], 0.0)

    def put_lambda():
        lv = lam[...]
        hi = lv.astype(BF16).astype(F32)
        r1 = lv - hi
        mid = r1.astype(BF16).astype(F32)
        lo = (r1 - mid).astype(BF16).astype(F32)
        for r in range(4 * XC):
            t = jnp.where(
                sub16 == 0, hi[r:r + 1, :],
                jnp.where(sub16 == 1, mid[r:r + 1, :],
                          jnp.where(sub16 == 2, lo[r:r + 1, :],
                                    jnp.where(sub16 == 3, 1.0, 0.0))))
            iaug[r // 4, 64:80, (r % 4) * 128:(r % 4 + 1) * 128] = t.astype(BF16)

    put_lambda()
    minus = jnp.where(sub64 < 3, -1.0, 0.0)

    def put_raw(b):
        for h in range(2):
            blk = ut[b, :, h * 128:(h + 1) * 128].astype(F32)
            rows = pl.ds(pl.multiple_of(b * 256 + h * 128, 128), 128)
            uraw[rows, :] = jnp.concatenate([blk, minus], axis=0).T.astype(BF16)

    put_raw(yl)
    pl.semaphore_wait(barrier, len(peers))

    pending = []
    gu = copies(ut.at[yl], ut.at[yl], gu_s, gu_r, lpeers)
    fwd, bwd = (x + 1) % X, (x + X - 1) % X
    opp = (x + 2) % X
    nxt, prv, other = dev(fwd, y, c, z), dev(bwd, y, c, z), dev(x, y, 1 - c, z)

    def items(x_, part=None):
        r = pl.ds(0, 64) if part is None else pl.ds(32 * part, 32)
        return iaug.at[x_ * C + c, r, :]

    def gsend(x_, part, k, target):
        q = send(items(x_, part), items(x_, part), gi_s.at[k], gi_r.at[k], target)
        pending.append(q)
        return q

    f0 = gsend(x, 0, 0, nxt)
    b1 = gsend(x, 1, 1, prv)
    own = gsend(x, None, 2, other)
    f1 = gsend(x, 1, 3, nxt)
    b0 = gsend(x, 0, 4, prv)
    f0.wait_recv()
    fo = gsend(bwd, 0, 5, nxt)
    b1.wait_recv()
    bo = gsend(fwd, 1, 6, prv)
    f1.wait_recv()
    cb = gsend(bwd, None, 7, other)
    b0.wait_recv()
    cf = gsend(fwd, None, 8, other)

    def put_users(muv):
        coef = owv + muv
        coef = jnp.where(lane < 64, coef, 1.0)
        for r in range(0, NU, 128):
            rows = slice(r, r + 128)
            sc = (uraw[rows, :].astype(F32) * coef).astype(BF16).astype(F32) * (1.0 / TAU)
            uaug[rows, :] = sc.astype(BF16)

    def logits(b, first):
        zt = jnp.dot(uaug[...], iaug[b], preferred_element_type=F32)
        zbuf[b] = zt
        m = jnp.maximum(jnp.maximum(zt[:, 0:128], zt[:, 128:256]),
                        jnp.maximum(zt[:, 256:384], zt[:, 384:512]))
        macc[...] = m if first else jnp.maximum(macc[...], m)

    def pass1_step(b, carry):
        logits(b, False)
        return carry

    def towers(e16, b):
        tacc[...] += lax.dot_general(
            e16, iaug[b], (((1,), (1,)), ((), ())), preferred_element_type=F32)

    def pass2_step(last, b, carry):
        mb = macc[...]
        parts = [jnp.exp(zbuf[b, :, k * 128:(k + 1) * 128] - mb) for k in range(4)]
        e16 = jnp.concatenate(parts, axis=1).astype(BF16)
        ebuf[b] = e16
        if last:
            sacc[...] += (parts[0] + parts[1]) + (parts[2] + parts[3])
        else:
            towers(e16, b)
        return carry

    def towers_step(b, carry):
        towers(ebuf[b], b)
        return carry

    def put_numerators(q, pt):
        uf = ut[q // 2, :, (q % 2) * 128:(q % 2 + 1) * 128].astype(F32)
        prod = uf * pt[0:64, :]
        for k in range(4):
            st[2 + k, q:q + 1, :] = jnp.sum(prod[16 * k:16 * k + 16, :], axis=0, keepdims=True)

    def lse(v):
        top = jnp.max(v, axis=0)
        return top + jnp.log(jnp.sum(jnp.exp(v - top[None]), axis=0))

    for it in range(ITERS):
        if it == 0:
            for q in gu:
                q.wait_recv()
            for d in range(1, YL):
                put_raw((yl + d) % YL)
            put_users(mu)
            logits(x * C + c, True)
            own.wait_recv()
            logits(x * C + 1 - c, False)
            logits(bwd * C + c, False)
            logits(fwd * C + c, False)
            fo.wait_recv()
            bo.wait_recv()
            co = gsend(opp, None, 9, other)
            cb.wait_recv()
            logits(bwd * C + 1 - c, False)
            cf.wait_recv()
            logits(fwd * C + 1 - c, False)
            logits(opp * C + c, False)
            co.wait_recv()
            logits(opp * C + 1 - c, False)
            pending += gu
        else:
            logits(0, True)
            lax.fori_loop(1, XC, pass1_step, 0, unroll=True)
        for q in range(NC):
            rows = slice(q * 128, (q + 1) * 128)
            m = jnp.max(macc[rows, :], axis=1, keepdims=True)
            macc[rows, :] = jnp.broadcast_to(m, (128, 128))
        last = it == ITERS - 1
        tacc[...] = jnp.zeros((NU, 128), F32)
        if last:
            sacc[...] = jnp.zeros((NU, 128), F32)

        lax.fori_loop(0, XC, functools.partial(pass2_step, last), 0, unroll=4)

        for q in range(NC):
            rows = slice(q * 128, (q + 1) * 128)
            if last:
                sv = sacc[rows, :]
                sv = sv + pltpu.roll(sv, 64, 1)
                pt = jnp.where(lane128 < 64, sv, macc[rows, :]).T
                st[1, q:q + 1, :] = jnp.sum(pt[0:64, :], axis=0, keepdims=True)
            else:
                pt = jnp.where(lane128 == 64, macc[rows, :], tacc[rows, :]).T
                st[1, q:q + 1, :] = pt[67:68, :]
                put_numerators(q, pt)
            st[0, q:q + 1, :] = pt[64:65, :]

        m_loc = st[0]
        s_loc = st[1]
        yll[it, y] = m_loc + jnp.log(s_loc)
        cy_l = copies(yll.at[it, y], yll.at[it, y], yl_s.at[it], yl_r.at[it], ypeers)
        inv = 1.0 / s_loc
        if last:
            lax.fori_loop(0, XC, towers_step, 0, unroll=4)
            for q in range(NC):
                put_numerators(q, tacc[q * 128:(q + 1) * 128, :].T)
        for k in range(4):
            yn[it, y, k] = st[2 + k] * inv
        cy_n = copies(yn.at[it, y], yn.at[it, y], yn_s.at[it], yn_r.at[it], ypeers)
        for q in cy_l:
            q.wait_recv()
        lv = yll[it]
        ly = lse(lv)
        zll[it, z] = ly
        cz_l = copies(zll.at[it, z], zll.at[it, z], zl_s.at[it], zl_r.at[it], zpeers)
        fy = jnp.exp(lv - ly[None])
        for q in cy_n:
            q.wait_recv()
        nv = yn[it]
        for k in range(4):
            zn[it, z, k] = jnp.sum(nv[:, k] * fy, axis=0)
        cz_n = copies(zn.at[it, z], zn.at[it, z], zn_s.at[it], zn_r.at[it], zpeers)
        for q in cz_l:
            q.wait_recv()
        lv = zll[it]
        lg = lse(lv)
        w = jnp.exp(m_loc - lg)
        if last:
            macc[0:NC, :] = TAU * lg
            out[rows_out:rows_out + 2, :] = macc[pl.ds(yl * 2, 2), :]
        whi = w.astype(BF16).astype(F32)
        r1 = w - whi
        wmid = r1.astype(BF16).astype(F32)
        wlo = (r1 - wmid).astype(BF16).astype(F32)
        for q in range(NC):
            t = jnp.where(
                sub16 == 0, whi[q:q + 1, :],
                jnp.where(sub16 == 1, wmid[q:q + 1, :],
                          jnp.where(sub16 == 2, wlo[q:q + 1, :], 0.0)))
            wl[:, q * 128:(q + 1) * 128] = t.astype(BF16)
        cx_l = []
        for h in range(2):
            for b in range(h * XC // 2, (h + 1) * XC // 2):
                acc = jnp.dot(wl[...], ebuf[b], preferred_element_type=F32)
                row = acc[0:1, :] + acc[1:2, :] + acc[2:3, :]
                for k in range(4):
                    xload[it, xc, 4 * b + k:4 * b + k + 1, :] = row[:, k * 128:(k + 1) * 128]
            part = xload.at[it, xc, pl.ds(2 * XC * h, 2 * XC), :]
            cx_l += copies(part, part, xl_s.at[it, h], xl_r.at[it, h], xpeers)
        fz = jnp.exp(lv - lg[None])
        for q in cz_n:
            q.wait_recv()
        nv = zn[it]
        xach[it, xc] = jnp.zeros((8, 128), F32)
        for k in range(4):
            t = jnp.sum(nv[:, k] * fz, axis=0)
            xach[it, xc, k:k + 1, :] = jnp.sum(t, axis=0, keepdims=True)
        cx_a = copies(xach.at[it, xc], xach.at[it, xc], xa_s.at[it], xa_r.at[it], xpeers)
        for q in cx_l:
            q.wait_recv()
        load = jnp.sum(xload[it], axis=0)
        lam[...] = jnp.maximum(
            0.0, lam[...] + DUAL_STEP * (load * (items_total / users_total) - capl[...]))
        if not last:
            put_lambda()
        else:
            agbuf[yl] = lam[...]
            ca = copies(agbuf.at[yl], agbuf.at[yl], ag_s, ag_r, lpeers)
        for q in cx_a:
            q.wait_recv()
        ach = jnp.sum(jnp.sum(xach[it], axis=0), axis=1, keepdims=True) / users_total
        achv = by_tower([ach[k:k + 1, :] for k in range(4)], 0.0)
        mu = mu + TARGET_STEP * (otv - achv)
        if not last:
            put_users(mu)
        pending += cy_l + cy_n + cz_l + cz_n + cx_l + cx_a

    out[rows_out + 2:rows_out + 3, :] = mu
    for q in ca:
        q.wait_recv()
    for l in range(YL):
        for xx in range(X):
            out[(xx * YL + l) * RX:(xx * YL + l + 1) * RX, :] = agbuf[l, xx * RX:(xx + 1) * RX, :]
    for q in pending + ca:
        q.wait_send()


def split_out(rows, packed, soft_out, cap_out, obj_out):
    cap_out[...] = packed[0:rows, :]
    soft_out[...] = packed[rows:rows + 2, :]
    lane = lax.broadcasted_iota(jnp.int32, (1, 128), 1)
    mu = packed[rows + 2:rows + 3, :]
    for k in range(4):
        obj_out[k] = jnp.max(jnp.where(lane == 16 * k, mu, -3.0e38))


def per_device(g, user_emb, item_emb, ow, ot, od, duals, cap):
    X, YL, C, YH, Z = g.X, g.YL, g.C, g.YH, g.Z
    Y, XC, NU = YL * YH, X * C, UD * YL
    NC = NU // 128
    rows = IB * X * YL * C // 128
    vm = pl.BlockSpec(memory_space=pltpu.VMEM)
    sm = pl.BlockSpec(memory_space=pltpu.SMEM)
    hbm = pl.BlockSpec(memory_space=pl.ANY)
    dma = pltpu.SemaphoreType.DMA
    V = pltpu.VMEM
    nl = max(YL - 1, 1)
    packed = pl.pallas_call(
        functools.partial(kernel, g),
        out_shape=jax.ShapeDtypeStruct((rows + 8, 128), F32),
        in_specs=[hbm] * 7,
        out_specs=vm,
        scratch_shapes=[
            pltpu.SMEM((4,), F32), pltpu.SMEM((4,), F32), pltpu.SMEM((4,), F32),
            V((YL, 64, UD), BF16),
            V((NU, KD), BF16),
            V((XC, KD, IB), BF16),
            V((NU, KD), BF16),
            V((XC, NU, IB), F32),
            V((XC, NU, IB), BF16),
            V((NU, 128), F32),
            V((NU, 128), F32),
            V((NU, 128), F32),
            V((6, NC, 128), F32),
            V((16, NU), BF16),
            V((4 * XC, 128), F32),
            V((4 * XC, 128), F32),
            V((ITERS, Y, NC, 128), F32),
            V((ITERS, Y, 4, NC, 128), F32),
            V((ITERS, Z, NC, 128), F32),
            V((ITERS, Z, 4, NC, 128), F32),
            V((ITERS, XC, 4 * XC, 128), F32),
            V((ITERS, XC, 8, 128), F32),
            V((YL, 4 * XC, 128), F32),
            dma((5 + 2 * X,)),
            dma((10,)), dma((10,)), dma((nl,)), dma((nl,)),
            dma((ITERS, Y - 1)), dma((ITERS, Y - 1)), dma((ITERS, Y - 1)), dma((ITERS, Y - 1)),
            dma((ITERS, Z - 1)), dma((ITERS, Z - 1)), dma((ITERS, Z - 1)), dma((ITERS, Z - 1)),
            dma((ITERS, 2, XC - 1)), dma((ITERS, 2, XC - 1)), dma((ITERS, XC - 1)), dma((ITERS, XC - 1)),
            dma((nl,)), dma((nl,)),
        ],
        compiler_params=pltpu.CompilerParams(
            collective_id=0, has_side_effects=True, vmem_limit_bytes=60 * 1024 * 1024),
        name="dual_ascent",
    )(user_emb.T, item_emb, duals.reshape(rows, 128), cap.reshape(rows, 128), ow, ot, od)
    soft, capo, obj = pl.pallas_call(
        functools.partial(split_out, rows),
        out_shape=(
            jax.ShapeDtypeStruct((UD // 128, 128), F32),
            jax.ShapeDtypeStruct((rows, 128), F32),
            jax.ShapeDtypeStruct((4,), F32),
        ),
        in_specs=[vm],
        out_specs=(vm, vm, sm),
        name="split_out",
    )(packed)
    return soft.reshape(UD), capo.reshape(rows * 128), obj


def solution(mesh, g=SLICE):
    in_specs = (P("user", None), P(None, ("item", "user")), P(), P(), P(), P("item"), P("item"))
    out_specs = (P("user"), P("item"), P())
    return jax.shard_map(
        functools.partial(per_device, g), mesh=mesh, in_specs=in_specs, out_specs=out_specs,
        check_vma=False,
    )
```

```python
import functools
from types import SimpleNamespace

import jax
import jax.numpy as jnp
from jax import lax
from jax.experimental import pallas as pl
from jax.experimental.pallas import tpu as pltpu
from jax.sharding import PartitionSpec as P

ITERS = 2
TAU = 2.0
DUAL_STEP = 0.5
TARGET_STEP = 4.0
MESH = pl.DeviceIdType.MESH

SLICE = SimpleNamespace(X=4, YL=4, C=2, YH=2, Z=8)

F32 = jnp.float32
BF16 = jnp.bfloat16
UD = 256
IB = 512
KD = 128


def kernel(
    g,
    user_hbm, item_hbm, duals_hbm, cap_hbm, ow_hbm, ot_hbm, od_hbm,
    out,
    ow_ref, ot_ref, od_ref,
    ut, uraw, iaug, uaug, zbuf, ebuf, macc, tacc, st, wl, lam, capl,
    yll, yn, zll, zn, xload, xach, agbuf,
    in_s, gi_s, gi_r, gu_s, gu_r,
    yl_s, yl_r, yn_s, yn_r, zl_s, zl_r, zn_s, zn_r,
    xl_s, xl_r, xa_s, xa_r, ag_s, ag_r,
):
    X, YL, C, YH, Z = g.X, g.YL, g.C, g.YH, g.Z
    Y, XC = YL * YH, X * C
    NU = UD * YL
    NC = NU // 128
    users_total = UD * X * YL * C
    items_total = IB * X * YL * C * YH * Z
    ui = lax.axis_index("user")
    ii = lax.axis_index("item")
    c = ui % C
    yl = (ui // C) % YL
    x = ui // (C * YL)
    yh = ii // Z
    z = ii % Z
    y = yh * YL + yl
    xc = x * C + c

    def dev(x_, y_, c_, z_):
        return ((x_ * YL + y_ % YL) * C + c_, (y_ // YL) * Z + z_)

    def far_first(n):
        return sorted(range(1, n), key=lambda d: -min(d, n - d))

    ypeers = [dev(x, (y + d) % Y, c, z) for d in far_first(Y)]
    zpeers = [dev(x, y, c, (z + d) % Z) for d in far_first(Z)]
    xpeers = [
        dev((x + dx) % X, y, (c + dc) % C, z)
        for dx in far_first(X) + [0] for dc in range(C) if (dx, dc) != (0, 0)
    ]
    lpeers = [dev(x, yh * YL + (yl + d) % YL, c, z) for d in range(1, YL)]

    barrier = pltpu.get_barrier_semaphore()
    peers = ypeers + zpeers + xpeers
    for p in peers:
        pl.semaphore_signal(barrier, inc=1, device_id=p, device_id_type=MESH)

    own_items = iaug.at[xc, pl.ds(0, 64), :]
    local = [
        pltpu.make_async_copy(user_hbm, ut.at[yl], in_s.at[0]),
        pltpu.make_async_copy(item_hbm, own_items, in_s.at[1]),
        pltpu.make_async_copy(ow_hbm, ow_ref, in_s.at[2]),
        pltpu.make_async_copy(ot_hbm, ot_ref, in_s.at[3]),
        pltpu.make_async_copy(od_hbm, od_ref, in_s.at[4]),
    ]
    RX = 4 * C
    rows_out = RX * X * YL
    for xx in range(X):
        rows = pl.ds(pl.multiple_of((xx * YL + yl) * RX, RX), RX)
        mine = pl.ds(xx * RX, RX)
        local.append(pltpu.make_async_copy(duals_hbm.at[rows], lam.at[mine], in_s.at[5 + 2 * xx]))
        local.append(pltpu.make_async_copy(cap_hbm.at[rows], capl.at[mine], in_s.at[6 + 2 * xx]))
    for q in local:
        q.start()
    for b in range(XC):
        iaug[b, 64:128, :] = jnp.zeros((64, IB), BF16)
    for q in local:
        q.wait()

    def send(src, dst, ss, rs, target):
        q = pltpu.make_async_remote_copy(
            src_ref=src, dst_ref=dst, send_sem=ss, recv_sem=rs,
            device_id=target, device_id_type=MESH)
        q.start()
        return q

    def copies(src, dst, ss, rs, targets):
        return [send(src, dst, ss.at[k], rs.at[k], t) for k, t in enumerate(targets)]

    lane = lax.broadcasted_iota(jnp.int32, (1, 128), 1)
    tower = lane // 16
    lane128 = lax.broadcasted_iota(jnp.int32, (128, 128), 1)
    sub16 = lax.broadcasted_iota(jnp.int32, (16, 128), 0)
    sub64 = lax.broadcasted_iota(jnp.int32, (64, 128), 0)

    def by_tower(vals, rest):
        out = jnp.full((1, 128), rest, F32)
        for k in range(4):
            out = jnp.where(tower == k, vals[k], out)
        return out

    owv = by_tower([ow_ref[k] for k in range(4)], 1.0)
    otv = by_tower([ot_ref[k] for k in range(4)], 0.0)
    mu = by_tower([od_ref[k] for k in range(4)], 0.0)

    def put_lambda():
        lv = lam[...]
        hi = lv.astype(BF16).astype(F32)
        r1 = lv - hi
        mid = r1.astype(BF16).astype(F32)
        lo = (r1 - mid).astype(BF16).astype(F32)
        for r in range(4 * XC):
            t = jnp.where(
                sub16 == 0, hi[r:r + 1, :],
                jnp.where(sub16 == 1, mid[r:r + 1, :],
                          jnp.where(sub16 == 2, lo[r:r + 1, :],
                                    jnp.where(sub16 == 3, 1.0, 0.0))))
            iaug[r // 4, 64:80, (r % 4) * 128:(r % 4 + 1) * 128] = t.astype(BF16)

    put_lambda()
    minus = jnp.where(sub64 < 3, -1.0, 0.0)

    def put_raw(b):
        for h in range(2):
            blk = ut[b, :, h * 128:(h + 1) * 128].astype(F32)
            rows = pl.ds(pl.multiple_of(b * 256 + h * 128, 128), 128)
            uraw[rows, :] = jnp.concatenate([blk, minus], axis=0).T.astype(BF16)

    put_raw(yl)
    pl.semaphore_wait(barrier, len(peers))

    pending = []
    gu = copies(ut.at[yl], ut.at[yl], gu_s, gu_r, lpeers)
    fwd, bwd = (x + 1) % X, (x + X - 1) % X
    opp = (x + 2) % X
    nxt, prv, other = dev(fwd, y, c, z), dev(bwd, y, c, z), dev(x, y, 1 - c, z)

    def items(x_, part=None):
        r = pl.ds(0, 64) if part is None else pl.ds(32 * part, 32)
        return iaug.at[x_ * C + c, r, :]

    def gsend(x_, part, k, target):
        q = send(items(x_, part), items(x_, part), gi_s.at[k], gi_r.at[k], target)
        pending.append(q)
        return q

    far = dev(opp, y, c, z)
    f0 = gsend(x, None, 0, nxt)
    b0 = gsend(x, None, 1, prv)
    fo = gsend(x, None, 3, far)
    own = gsend(x, None, 2, other)
    f0.wait_recv()
    cb = gsend(bwd, None, 7, other)
    b0.wait_recv()
    cf = gsend(fwd, None, 8, other)

    def put_users(muv):
        coef = owv + muv
        coef = jnp.where(lane < 64, coef, 1.0)
        for r in range(0, NU, 128):
            rows = slice(r, r + 128)
            sc = (uraw[rows, :].astype(F32) * coef).astype(BF16).astype(F32) * (1.0 / TAU)
            uaug[rows, :] = sc.astype(BF16)

    def logits(b, first):
        zt = jnp.dot(uaug[...], iaug[b], preferred_element_type=F32)
        zbuf[b] = zt
        m = jnp.maximum(jnp.maximum(zt[:, 0:128], zt[:, 128:256]),
                        jnp.maximum(zt[:, 256:384], zt[:, 384:512]))
        macc[...] = m if first else jnp.maximum(macc[...], m)

    def pass1_step(b, carry):
        logits(b, False)
        return carry

    def pass2_step(b, carry):
        mb = macc[...]
        parts = [jnp.exp(zbuf[b, :, k * 128:(k + 1) * 128] - mb) for k in range(4)]
        e16 = jnp.concatenate(parts, axis=1).astype(BF16)
        ebuf[b] = e16
        tacc[...] += lax.dot_general(
            e16, iaug[b], (((1,), (1,)), ((), ())), preferred_element_type=F32)
        return carry

    def put_numerators(q, pt):
        uf = ut[q // 2, :, (q % 2) * 128:(q % 2 + 1) * 128].astype(F32)
        prod = uf * pt[0:64, :]
        for k in range(4):
            st[2 + k, q:q + 1, :] = jnp.sum(prod[16 * k:16 * k + 16, :], axis=0, keepdims=True)

    def lse(v):
        top = jnp.max(v, axis=0)
        return top + jnp.log(jnp.sum(jnp.exp(v - top[None]), axis=0))

    for it in range(ITERS):
        if it == 0:
            for q in gu:
                q.wait_recv()
            for d in range(1, YL):
                put_raw((yl + d) % YL)
            put_users(mu)
            logits(x * C + c, True)
            own.wait_recv()
            logits(x * C + 1 - c, False)
            logits(bwd * C + c, False)
            logits(fwd * C + c, False)
            fo.wait_recv()
            co = gsend(opp, None, 9, other)
            cb.wait_recv()
            logits(bwd * C + 1 - c, False)
            cf.wait_recv()
            logits(fwd * C + 1 - c, False)
            logits(opp * C + c, False)
            co.wait_recv()
            logits(opp * C + 1 - c, False)
            pending += gu
        else:
            logits(0, True)
            lax.fori_loop(1, XC, pass1_step, 0, unroll=True)
        for q in range(NC):
            rows = slice(q * 128, (q + 1) * 128)
            m = jnp.max(macc[rows, :], axis=1, keepdims=True)
            macc[rows, :] = jnp.broadcast_to(m, (128, 128))
        last = it == ITERS - 1
        tacc[...] = jnp.zeros((NU, 128), F32)

        lax.fori_loop(0, XC, pass2_step, 0, unroll=4)

        for q in range(NC):
            rows = slice(q * 128, (q + 1) * 128)
            pt = jnp.where(lane128 == 64, macc[rows, :], tacc[rows, :]).T
            st[1, q:q + 1, :] = pt[67:68, :]
            put_numerators(q, pt)
            st[0, q:q + 1, :] = pt[64:65, :]

        m_loc = st[0]
        s_loc = st[1]
        yll[it, y] = m_loc + jnp.log(s_loc)
        cy_l = copies(yll.at[it, y], yll.at[it, y], yl_s.at[it], yl_r.at[it], ypeers)
        inv = 1.0 / s_loc
        for k in range(4):
            yn[it, y, k] = st[2 + k] * inv
        cy_n = copies(yn.at[it, y], yn.at[it, y], yn_s.at[it], yn_r.at[it], ypeers)
        for q in cy_l:
            q.wait_recv()
        lv = yll[it]
        ly = lse(lv)
        zll[it, z] = ly
        cz_l = copies(zll.at[it, z], zll.at[it, z], zl_s.at[it], zl_r.at[it], zpeers)
        fy = jnp.exp(lv - ly[None])
        for q in cy_n:
            q.wait_recv()
        nv = yn[it]
        for k in range(4):
            zn[it, z, k] = jnp.sum(nv[:, k] * fy, axis=0)
        cz_n = copies(zn.at[it, z], zn.at[it, z], zn_s.at[it], zn_r.at[it], zpeers)
        for q in cz_l:
            q.wait_recv()
        lv = zll[it]
        lg = lse(lv)
        w = jnp.exp(m_loc - lg)
        if last:
            macc[0:NC, :] = TAU * lg
            out[rows_out:rows_out + 2, :] = macc[pl.ds(yl * 2, 2), :]
        whi = w.astype(BF16).astype(F32)
        r1 = w - whi
        wmid = r1.astype(BF16).astype(F32)
        wlo = (r1 - wmid).astype(BF16).astype(F32)
        for q in range(NC):
            t = jnp.where(
                sub16 == 0, whi[q:q + 1, :],
                jnp.where(sub16 == 1, wmid[q:q + 1, :],
                          jnp.where(sub16 == 2, wlo[q:q + 1, :], 0.0)))
            wl[:, q * 128:(q + 1) * 128] = t.astype(BF16)
        for b in range(XC):
            acc = jnp.dot(wl[...], ebuf[b], preferred_element_type=F32)
            row = acc[0:1, :] + acc[1:2, :] + acc[2:3, :]
            for k in range(4):
                xload[it, xc, 4 * b + k:4 * b + k + 1, :] = row[:, k * 128:(k + 1) * 128]
        cx_l = copies(xload.at[it, xc], xload.at[it, xc], xl_s.at[it], xl_r.at[it], xpeers)
        fz = jnp.exp(lv - lg[None])

        def loads_in():
            for q in cx_l:
                q.wait_recv()
            load = jnp.sum(xload[it], axis=0)
            lam[...] = jnp.maximum(
                0.0, lam[...] + DUAL_STEP * (load * (items_total / users_total) - capl[...]))

        if last:
            loads_in()
            agbuf[yl] = lam[...]
            ca = copies(agbuf.at[yl], agbuf.at[yl], ag_s, ag_r, lpeers)
        for q in cz_n:
            q.wait_recv()
        nv = zn[it]
        xach[it, xc] = jnp.zeros((8, 128), F32)
        for k in range(4):
            t = jnp.sum(nv[:, k] * fz, axis=0)
            xach[it, xc, k:k + 1, :] = jnp.sum(t, axis=0, keepdims=True)
        cx_a = copies(xach.at[it, xc], xach.at[it, xc], xa_s.at[it], xa_r.at[it], xpeers)
        if not last:
            loads_in()
            put_lambda()
        for q in cx_a:
            q.wait_recv()
        ach = jnp.sum(jnp.sum(xach[it], axis=0), axis=1, keepdims=True) / users_total
        achv = by_tower([ach[k:k + 1, :] for k in range(4)], 0.0)
        mu = mu + TARGET_STEP * (otv - achv)
        if not last:
            put_users(mu)
        pending += cy_l + cy_n + cz_l + cz_n + cx_l + cx_a

    out[rows_out + 2:rows_out + 3, :] = mu
    for q in ca:
        q.wait_recv()
    for l in range(YL):
        for xx in range(X):
            out[(xx * YL + l) * RX:(xx * YL + l + 1) * RX, :] = agbuf[l, xx * RX:(xx + 1) * RX, :]
    for q in pending + ca:
        q.wait_send()


def split_out(rows, packed, soft_out, cap_out, obj_out):
    cap_out[...] = packed[0:rows, :]
    soft_out[...] = packed[rows:rows + 2, :]
    lane = lax.broadcasted_iota(jnp.int32, (1, 128), 1)
    mu = packed[rows + 2:rows + 3, :]
    for k in range(4):
        obj_out[k] = jnp.max(jnp.where(lane == 16 * k, mu, -3.0e38))


def per_device(g, user_emb, item_emb, ow, ot, od, duals, cap):
    X, YL, C, YH, Z = g.X, g.YL, g.C, g.YH, g.Z
    Y, XC, NU = YL * YH, X * C, UD * YL
    NC = NU // 128
    rows = IB * X * YL * C // 128
    vm = pl.BlockSpec(memory_space=pltpu.VMEM)
    sm = pl.BlockSpec(memory_space=pltpu.SMEM)
    hbm = pl.BlockSpec(memory_space=pl.ANY)
    dma = pltpu.SemaphoreType.DMA
    V = pltpu.VMEM
    nl = max(YL - 1, 1)
    packed = pl.pallas_call(
        functools.partial(kernel, g),
        out_shape=jax.ShapeDtypeStruct((rows + 8, 128), F32),
        in_specs=[hbm] * 7,
        out_specs=vm,
        scratch_shapes=[
            pltpu.SMEM((4,), F32), pltpu.SMEM((4,), F32), pltpu.SMEM((4,), F32),
            V((YL, 64, UD), BF16),
            V((NU, KD), BF16),
            V((XC, KD, IB), BF16),
            V((NU, KD), BF16),
            V((XC, NU, IB), F32),
            V((XC, NU, IB), BF16),
            V((NU, 128), F32),
            V((NU, 128), F32),
            V((6, NC, 128), F32),
            V((16, NU), BF16),
            V((4 * XC, 128), F32),
            V((4 * XC, 128), F32),
            V((ITERS, Y, NC, 128), F32),
            V((ITERS, Y, 4, NC, 128), F32),
            V((ITERS, Z, NC, 128), F32),
            V((ITERS, Z, 4, NC, 128), F32),
            V((ITERS, XC, 4 * XC, 128), F32),
            V((ITERS, XC, 8, 128), F32),
            V((YL, 4 * XC, 128), F32),
            dma((5 + 2 * X,)),
            dma((10,)), dma((10,)), dma((nl,)), dma((nl,)),
            dma((ITERS, Y - 1)), dma((ITERS, Y - 1)), dma((ITERS, Y - 1)), dma((ITERS, Y - 1)),
            dma((ITERS, Z - 1)), dma((ITERS, Z - 1)), dma((ITERS, Z - 1)), dma((ITERS, Z - 1)),
            dma((ITERS, XC - 1)), dma((ITERS, XC - 1)), dma((ITERS, XC - 1)), dma((ITERS, XC - 1)),
            dma((nl,)), dma((nl,)),
        ],
        compiler_params=pltpu.CompilerParams(
            collective_id=0, has_side_effects=True, vmem_limit_bytes=60 * 1024 * 1024),
        name="dual_ascent",
    )(user_emb.T, item_emb, duals.reshape(rows, 128), cap.reshape(rows, 128), ow, ot, od)
    soft, capo, obj = pl.pallas_call(
        functools.partial(split_out, rows),
        out_shape=(
            jax.ShapeDtypeStruct((UD // 128, 128), F32),
            jax.ShapeDtypeStruct((rows, 128), F32),
            jax.ShapeDtypeStruct((4,), F32),
        ),
        in_specs=[vm],
        out_specs=(vm, vm, sm),
        name="split_out",
    )(packed)
    return soft.reshape(UD), capo.reshape(rows * 128), obj


def solution(mesh, g=SLICE):
    in_specs = (P("user", None), P(None, ("item", "user")), P(), P(), P(), P("item"), P("item"))
    out_specs = (P("user"), P("item"), P())
    return jax.shard_map(
        functools.partial(per_device, g), mesh=mesh, in_specs=in_specs, out_specs=out_specs,
        check_vma=False,
    )
```

```python
import functools
from types import SimpleNamespace

import jax
import jax.numpy as jnp
from jax import lax
from jax.experimental import pallas as pl
from jax.experimental.pallas import tpu as pltpu
from jax.sharding import PartitionSpec as P

ITERS = 2
TAU = 2.0
DUAL_STEP = 0.5
TARGET_STEP = 4.0
MESH = pl.DeviceIdType.MESH

SLICE = SimpleNamespace(X=4, YL=4, C=2, YH=2, Z=8)

F32 = jnp.float32
BF16 = jnp.bfloat16
UD = 256
IB = 512
KD = 128


def kernel(
    g,
    user_hbm, item_hbm, duals_hbm, cap_hbm, ow_hbm, ot_hbm, od_hbm,
    out,
    ow_ref, ot_ref, od_ref,
    ut, uraw, iaug, uaug, zbuf, ebuf, macc, tacc, st, wl, lam, capl,
    yll, yn, zll, zn, xload, xach, agbuf,
    in_s, gi_s, gi_r, gu_s, gu_r,
    yl_s, yl_r, yn_s, yn_r, zl_s, zl_r, zn_s, zn_r,
    xl_s, xl_r, xa_s, xa_r, ag_s, ag_r,
):
    X, YL, C, YH, Z = g.X, g.YL, g.C, g.YH, g.Z
    Y, XC = YL * YH, X * C
    NU = UD * YL
    NC = NU // 128
    users_total = UD * X * YL * C
    items_total = IB * X * YL * C * YH * Z
    ui = lax.axis_index("user")
    ii = lax.axis_index("item")
    c = ui % C
    yl = (ui // C) % YL
    x = ui // (C * YL)
    yh = ii // Z
    z = ii % Z
    y = yh * YL + yl
    xc = x * C + c

    def dev(x_, y_, c_, z_):
        return ((x_ * YL + y_ % YL) * C + c_, (y_ // YL) * Z + z_)

    def far_first(n):
        return sorted(range(1, n), key=lambda d: -min(d, n - d))

    ypeers = [dev(x, (y + d) % Y, c, z) for d in far_first(Y)]
    zpeers = [dev(x, y, c, (z + d) % Z) for d in far_first(Z)]
    xpeers = [
        dev((x + dx) % X, y, (c + dc) % C, z)
        for dx in far_first(X) + [0] for dc in range(C) if (dx, dc) != (0, 0)
    ]
    lpeers = [dev(x, yh * YL + (yl + d) % YL, c, z) for d in range(1, YL)]

    barrier = pltpu.get_barrier_semaphore()
    peers = ypeers + zpeers + xpeers
    for p in peers:
        pl.semaphore_signal(barrier, inc=1, device_id=p, device_id_type=MESH)

    own_items = iaug.at[xc, pl.ds(0, 64), :]
    local = [
        pltpu.make_async_copy(user_hbm, ut.at[yl], in_s.at[0]),
        pltpu.make_async_copy(item_hbm, own_items, in_s.at[1]),
        pltpu.make_async_copy(ow_hbm, ow_ref, in_s.at[2]),
        pltpu.make_async_copy(ot_hbm, ot_ref, in_s.at[3]),
        pltpu.make_async_copy(od_hbm, od_ref, in_s.at[4]),
    ]
    RX = 4 * C
    rows_out = RX * X * YL
    for xx in range(X):
        rows = pl.ds(pl.multiple_of((xx * YL + yl) * RX, RX), RX)
        mine = pl.ds(xx * RX, RX)
        local.append(pltpu.make_async_copy(duals_hbm.at[rows], lam.at[mine], in_s.at[5 + 2 * xx]))
        local.append(pltpu.make_async_copy(cap_hbm.at[rows], capl.at[mine], in_s.at[6 + 2 * xx]))
    for q in local:
        q.start()
    for b in range(XC):
        iaug[b, 64:128, :] = jnp.zeros((64, IB), BF16)
    for q in local[:2]:
        q.wait()

    def send(src, dst, ss, rs, target):
        q = pltpu.make_async_remote_copy(
            src_ref=src, dst_ref=dst, send_sem=ss, recv_sem=rs,
            device_id=target, device_id_type=MESH)
        q.start()
        return q

    def copies(src, dst, ss, rs, targets):
        return [send(src, dst, ss.at[k], rs.at[k], t) for k, t in enumerate(targets)]

    pl.semaphore_wait(barrier, len(peers))

    pending = []
    gu = copies(ut.at[yl], ut.at[yl], gu_s, gu_r, lpeers)
    fwd, bwd = (x + 1) % X, (x + X - 1) % X
    opp = (x + 2) % X
    nxt, prv, other = dev(fwd, y, c, z), dev(bwd, y, c, z), dev(x, y, 1 - c, z)

    def items(x_, part=None):
        r = pl.ds(0, 64) if part is None else pl.ds(32 * part, 32)
        return iaug.at[x_ * C + c, r, :]

    def gsend(x_, part, k, target):
        q = send(items(x_, part), items(x_, part), gi_s.at[k], gi_r.at[k], target)
        pending.append(q)
        return q

    far = dev(opp, y, c, z)
    fo = gsend(x, None, 3, far)
    f0 = gsend(x, None, 0, nxt)
    b0 = gsend(x, None, 1, prv)
    own = gsend(x, None, 2, other)

    lane = lax.broadcasted_iota(jnp.int32, (1, 128), 1)
    tower = lane // 16
    lane128 = lax.broadcasted_iota(jnp.int32, (128, 128), 1)
    sub16 = lax.broadcasted_iota(jnp.int32, (16, 128), 0)
    sub64 = lax.broadcasted_iota(jnp.int32, (64, 128), 0)

    def by_tower(vals, rest):
        out = jnp.full((1, 128), rest, F32)
        for k in range(4):
            out = jnp.where(tower == k, vals[k], out)
        return out

    for q in local[2:]:
        q.wait()
    owv = by_tower([ow_ref[k] for k in range(4)], 1.0)
    otv = by_tower([ot_ref[k] for k in range(4)], 0.0)
    mu = by_tower([od_ref[k] for k in range(4)], 0.0)

    def put_lambda():
        lv = lam[...]
        hi = lv.astype(BF16).astype(F32)
        r1 = lv - hi
        mid = r1.astype(BF16).astype(F32)
        lo = (r1 - mid).astype(BF16).astype(F32)
        for r in range(4 * XC):
            t = jnp.where(
                sub16 == 0, hi[r:r + 1, :],
                jnp.where(sub16 == 1, mid[r:r + 1, :],
                          jnp.where(sub16 == 2, lo[r:r + 1, :],
                                    jnp.where(sub16 == 3, 1.0, 0.0))))
            iaug[r // 4, 64:80, (r % 4) * 128:(r % 4 + 1) * 128] = t.astype(BF16)

    put_lambda()
    minus = jnp.where(sub64 < 3, -1.0, 0.0)

    def put_raw(b):
        for h in range(2):
            blk = ut[b, :, h * 128:(h + 1) * 128].astype(F32)
            rows = pl.ds(pl.multiple_of(b * 256 + h * 128, 128), 128)
            uraw[rows, :] = jnp.concatenate([blk, minus], axis=0).T.astype(BF16)

    put_raw(yl)

    b0.wait_recv()
    cf = gsend(fwd, None, 8, other)

    def put_users(muv):
        coef = owv + muv
        coef = jnp.where(lane < 64, coef, 1.0)
        for r in range(0, NU, 128):
            rows = slice(r, r + 128)
            sc = (uraw[rows, :].astype(F32) * coef).astype(BF16).astype(F32) * (1.0 / TAU)
            uaug[rows, :] = sc.astype(BF16)

    def logits(b, first):
        zt = jnp.dot(uaug[...], iaug[b], preferred_element_type=F32)
        zbuf[b] = zt
        m = jnp.maximum(jnp.maximum(zt[:, 0:128], zt[:, 128:256]),
                        jnp.maximum(zt[:, 256:384], zt[:, 384:512]))
        macc[...] = m if first else jnp.maximum(macc[...], m)

    def pass1_step(b, carry):
        logits(b, False)
        return carry

    def pass2_step(b, carry):
        mb = macc[...]
        parts = [jnp.exp(zbuf[b, :, k * 128:(k + 1) * 128] - mb) for k in range(4)]
        e16 = jnp.concatenate(parts, axis=1).astype(BF16)
        ebuf[b] = e16
        tacc[...] += lax.dot_general(
            e16, iaug[b], (((1,), (1,)), ((), ())), preferred_element_type=F32)
        return carry

    def put_numerators(q, pt):
        uf = ut[q // 2, :, (q % 2) * 128:(q % 2 + 1) * 128].astype(F32)
        prod = uf * pt[0:64, :]
        for k in range(4):
            st[2 + k, q:q + 1, :] = jnp.sum(prod[16 * k:16 * k + 16, :], axis=0, keepdims=True)

    def lse(v):
        top = jnp.max(v, axis=0)
        return top + jnp.log(jnp.sum(jnp.exp(v - top[None]), axis=0))

    for it in range(ITERS):
        if it == 0:
            for q in gu:
                q.wait_recv()
            for d in range(1, YL):
                put_raw((yl + d) % YL)
            put_users(mu)
            logits(x * C + c, True)
            fo.wait_recv()
            co = gsend(opp, None, 9, other)
            own.wait_recv()
            logits(x * C + 1 - c, False)
            f0.wait_recv()
            cb = gsend(bwd, None, 7, other)
            logits(fwd * C + c, False)
            cf.wait_recv()
            logits(fwd * C + 1 - c, False)
            logits(opp * C + c, False)
            logits(bwd * C + c, False)
            co.wait_recv()
            logits(opp * C + 1 - c, False)
            cb.wait_recv()
            logits(bwd * C + 1 - c, False)
            pending += gu
        else:
            logits(0, True)
            lax.fori_loop(1, XC, pass1_step, 0, unroll=True)
        for q in range(NC):
            rows = slice(q * 128, (q + 1) * 128)
            m = jnp.max(macc[rows, :], axis=1, keepdims=True)
            macc[rows, :] = jnp.broadcast_to(m, (128, 128))
        last = it == ITERS - 1
        tacc[...] = jnp.zeros((NU, 128), F32)

        lax.fori_loop(0, XC, pass2_step, 0, unroll=4)

        for q in range(NC):
            rows = slice(q * 128, (q + 1) * 128)
            pt = jnp.where(lane128 == 64, macc[rows, :], tacc[rows, :]).T
            st[1, q:q + 1, :] = pt[67:68, :]
            put_numerators(q, pt)
            st[0, q:q + 1, :] = pt[64:65, :]

        m_loc = st[0]
        s_loc = st[1]
        yll[it, y] = m_loc + jnp.log(s_loc)
        cy_l = copies(yll.at[it, y], yll.at[it, y], yl_s.at[it], yl_r.at[it], ypeers)
        inv = 1.0 / s_loc
        for k in range(4):
            yn[it, y, k] = st[2 + k] * inv
        cy_n = copies(yn.at[it, y], yn.at[it, y], yn_s.at[it], yn_r.at[it], ypeers)
        for q in cy_l:
            q.wait_recv()
        lv = yll[it]
        ly = lse(lv)
        zll[it, z] = ly
        cz_l = copies(zll.at[it, z], zll.at[it, z], zl_s.at[it], zl_r.at[it], zpeers)
        fy = jnp.exp(lv - ly[None])
        for q in cy_n:
            q.wait_recv()
        nv = yn[it]
        for k in range(4):
            zn[it, z, k] = jnp.sum(nv[:, k] * fy, axis=0)
        cz_n = copies(zn.at[it, z], zn.at[it, z], zn_s.at[it], zn_r.at[it], zpeers)
        for q in cz_l:
            q.wait_recv()
        lv = zll[it]
        lg = lse(lv)
        w = jnp.exp(m_loc - lg)
        if last:
            macc[0:NC, :] = TAU * lg
            out[rows_out:rows_out + 2, :] = macc[pl.ds(yl * 2, 2), :]
        whi = w.astype(BF16).astype(F32)
        r1 = w - whi
        wmid = r1.astype(BF16).astype(F32)
        wlo = (r1 - wmid).astype(BF16).astype(F32)
        for q in range(NC):
            t = jnp.where(
                sub16 == 0, whi[q:q + 1, :],
                jnp.where(sub16 == 1, wmid[q:q + 1, :],
                          jnp.where(sub16 == 2, wlo[q:q + 1, :], 0.0)))
            wl[:, q * 128:(q + 1) * 128] = t.astype(BF16)
        for b in range(XC):
            acc = jnp.dot(wl[...], ebuf[b], preferred_element_type=F32)
            row = acc[0:1, :] + acc[1:2, :] + acc[2:3, :]
            for k in range(4):
                xload[it, xc, 4 * b + k:4 * b + k + 1, :] = row[:, k * 128:(k + 1) * 128]
        cx_l = copies(xload.at[it, xc], xload.at[it, xc], xl_s.at[it], xl_r.at[it], xpeers)
        fz = jnp.exp(lv - lg[None])

        def loads_in():
            for q in cx_l:
                q.wait_recv()
            load = jnp.sum(xload[it], axis=0)
            lam[...] = jnp.maximum(
                0.0, lam[...] + DUAL_STEP * (load * (items_total / users_total) - capl[...]))

        if last:
            loads_in()
            agbuf[yl] = lam[...]
            ca = copies(agbuf.at[yl], agbuf.at[yl], ag_s, ag_r, lpeers)
        for q in cz_n:
            q.wait_recv()
        nv = zn[it]
        xach[it, xc] = jnp.zeros((8, 128), F32)
        for k in range(4):
            t = jnp.sum(nv[:, k] * fz, axis=0)
            xach[it, xc, k:k + 1, :] = jnp.sum(t, axis=0, keepdims=True)
        cx_a = copies(xach.at[it, xc], xach.at[it, xc], xa_s.at[it], xa_r.at[it], xpeers)
        if not last:
            loads_in()
            put_lambda()
        for q in cx_a:
            q.wait_recv()
        ach = jnp.sum(jnp.sum(xach[it], axis=0), axis=1, keepdims=True) / users_total
        achv = by_tower([ach[k:k + 1, :] for k in range(4)], 0.0)
        mu = mu + TARGET_STEP * (otv - achv)
        if not last:
            put_users(mu)
        pending += cy_l + cy_n + cz_l + cz_n + cx_l + cx_a

    out[rows_out + 2:rows_out + 3, :] = mu
    for q in ca:
        q.wait_recv()
    for l in range(YL):
        for xx in range(X):
            out[(xx * YL + l) * RX:(xx * YL + l + 1) * RX, :] = agbuf[l, xx * RX:(xx + 1) * RX, :]
    for q in pending + ca:
        q.wait_send()


def split_out(rows, packed, soft_out, cap_out, obj_out):
    cap_out[...] = packed[0:rows, :]
    soft_out[...] = packed[rows:rows + 2, :]
    lane = lax.broadcasted_iota(jnp.int32, (1, 128), 1)
    mu = packed[rows + 2:rows + 3, :]
    for k in range(4):
        obj_out[k] = jnp.max(jnp.where(lane == 16 * k, mu, -3.0e38))


def per_device(g, user_emb, item_emb, ow, ot, od, duals, cap):
    X, YL, C, YH, Z = g.X, g.YL, g.C, g.YH, g.Z
    Y, XC, NU = YL * YH, X * C, UD * YL
    NC = NU // 128
    rows = IB * X * YL * C // 128
    vm = pl.BlockSpec(memory_space=pltpu.VMEM)
    sm = pl.BlockSpec(memory_space=pltpu.SMEM)
    hbm = pl.BlockSpec(memory_space=pl.ANY)
    dma = pltpu.SemaphoreType.DMA
    V = pltpu.VMEM
    nl = max(YL - 1, 1)
    packed = pl.pallas_call(
        functools.partial(kernel, g),
        out_shape=jax.ShapeDtypeStruct((rows + 8, 128), F32),
        in_specs=[hbm] * 7,
        out_specs=vm,
        scratch_shapes=[
            pltpu.SMEM((4,), F32), pltpu.SMEM((4,), F32), pltpu.SMEM((4,), F32),
            V((YL, 64, UD), BF16),
            V((NU, KD), BF16),
            V((XC, KD, IB), BF16),
            V((NU, KD), BF16),
            V((XC, NU, IB), F32),
            V((XC, NU, IB), BF16),
            V((NU, 128), F32),
            V((NU, 128), F32),
            V((6, NC, 128), F32),
            V((16, NU), BF16),
            V((4 * XC, 128), F32),
            V((4 * XC, 128), F32),
            V((ITERS, Y, NC, 128), F32),
            V((ITERS, Y, 4, NC, 128), F32),
            V((ITERS, Z, NC, 128), F32),
            V((ITERS, Z, 4, NC, 128), F32),
            V((ITERS, XC, 4 * XC, 128), F32),
            V((ITERS, XC, 8, 128), F32),
            V((YL, 4 * XC, 128), F32),
            dma((5 + 2 * X,)),
            dma((10,)), dma((10,)), dma((nl,)), dma((nl,)),
            dma((ITERS, Y - 1)), dma((ITERS, Y - 1)), dma((ITERS, Y - 1)), dma((ITERS, Y - 1)),
            dma((ITERS, Z - 1)), dma((ITERS, Z - 1)), dma((ITERS, Z - 1)), dma((ITERS, Z - 1)),
            dma((ITERS, XC - 1)), dma((ITERS, XC - 1)), dma((ITERS, XC - 1)), dma((ITERS, XC - 1)),
            dma((nl,)), dma((nl,)),
        ],
        compiler_params=pltpu.CompilerParams(
            collective_id=0, has_side_effects=True, vmem_limit_bytes=60 * 1024 * 1024),
        name="dual_ascent",
    )(user_emb.T, item_emb, duals.reshape(rows, 128), cap.reshape(rows, 128), ow, ot, od)
    soft, capo, obj = pl.pallas_call(
        functools.partial(split_out, rows),
        out_shape=(
            jax.ShapeDtypeStruct((UD // 128, 128), F32),
            jax.ShapeDtypeStruct((rows, 128), F32),
            jax.ShapeDtypeStruct((4,), F32),
        ),
        in_specs=[vm],
        out_specs=(vm, vm, sm),
        name="split_out",
    )(packed)
    return soft.reshape(UD), capo.reshape(rows * 128), obj


def solution(mesh, g=SLICE):
    in_specs = (P("user", None), P(None, ("item", "user")), P(), P(), P(), P("item"), P("item"))
    out_specs = (P("user"), P("item"), P())
    return jax.shard_map(
        functools.partial(per_device, g), mesh=mesh, in_specs=in_specs, out_specs=out_specs,
        check_vma=False,
    )
```

```python
import functools
from types import SimpleNamespace

import jax
import jax.numpy as jnp
from jax import lax
from jax.experimental import pallas as pl
from jax.experimental.pallas import tpu as pltpu
from jax.sharding import PartitionSpec as P

ITERS = 2
TAU = 2.0
DUAL_STEP = 0.5
TARGET_STEP = 4.0
MESH = pl.DeviceIdType.MESH

SLICE = SimpleNamespace(X=4, YL=4, C=2, YH=2, Z=8)

F32 = jnp.float32
BF16 = jnp.bfloat16
UD = 256
IB = 512
KD = 128


def kernel(
    g,
    user_hbm, item_hbm, duals_hbm, cap_hbm, ow_hbm, ot_hbm, od_hbm,
    out,
    ow_ref, ot_ref, od_ref,
    ut, uraw, iaug, uaug, zbuf, ebuf, macc, tacc, ptn, st, wl, lam, capl,
    yll, yn, zll, zn, xload, xach, agbuf,
    in_s, gi_s, gi_r, gu_s, gu_r,
    yl_s, yl_r, yn_s, yn_r, zl_s, zl_r, zn_s, zn_r,
    xl_s, xl_r, xa_s, xa_r, ag_s, ag_r,
):
    X, YL, C, YH, Z = g.X, g.YL, g.C, g.YH, g.Z
    Y, XC = YL * YH, X * C
    NU = UD * YL
    NC = NU // 128
    users_total = UD * X * YL * C
    items_total = IB * X * YL * C * YH * Z
    ui = lax.axis_index("user")
    ii = lax.axis_index("item")
    c = ui % C
    yl = (ui // C) % YL
    x = ui // (C * YL)
    yh = ii // Z
    z = ii % Z
    y = yh * YL + yl
    xc = x * C + c

    def dev(x_, y_, c_, z_):
        return ((x_ * YL + y_ % YL) * C + c_, (y_ // YL) * Z + z_)

    def far_first(n):
        return sorted(range(1, n), key=lambda d: -min(d, n - d))

    ypeers = [dev(x, (y + d) % Y, c, z) for d in far_first(Y)]
    zpeers = [dev(x, y, c, (z + d) % Z) for d in far_first(Z)]
    xpeers = [
        dev((x + dx) % X, y, (c + dc) % C, z)
        for dx in far_first(X) + [0] for dc in range(C) if (dx, dc) != (0, 0)
    ]
    lpeers = [dev(x, yh * YL + (yl + d) % YL, c, z) for d in range(1, YL)]

    barrier = pltpu.get_barrier_semaphore()
    peers = ypeers + zpeers + xpeers
    for p in peers:
        pl.semaphore_signal(barrier, inc=1, device_id=p, device_id_type=MESH)

    own_items = iaug.at[xc, pl.ds(0, 64), :]
    local = [
        pltpu.make_async_copy(user_hbm, ut.at[yl], in_s.at[0]),
        pltpu.make_async_copy(item_hbm, own_items, in_s.at[1]),
        pltpu.make_async_copy(ow_hbm, ow_ref, in_s.at[2]),
        pltpu.make_async_copy(ot_hbm, ot_ref, in_s.at[3]),
        pltpu.make_async_copy(od_hbm, od_ref, in_s.at[4]),
    ]
    RX = 4 * C
    rows_out = RX * X * YL
    for xx in range(X):
        rows = pl.ds(pl.multiple_of((xx * YL + yl) * RX, RX), RX)
        mine = pl.ds(xx * RX, RX)
        local.append(pltpu.make_async_copy(duals_hbm.at[rows], lam.at[mine], in_s.at[5 + 2 * xx]))
        local.append(pltpu.make_async_copy(cap_hbm.at[rows], capl.at[mine], in_s.at[6 + 2 * xx]))
    for q in local:
        q.start()
    for b in range(XC):
        iaug[b, 64:128, :] = jnp.zeros((64, IB), BF16)
    for q in local[:2]:
        q.wait()

    def send(src, dst, ss, rs, target):
        q = pltpu.make_async_remote_copy(
            src_ref=src, dst_ref=dst, send_sem=ss, recv_sem=rs,
            device_id=target, device_id_type=MESH)
        q.start()
        return q

    def copies(src, dst, ss, rs, targets):
        return [send(src, dst, ss.at[k], rs.at[k], t) for k, t in enumerate(targets)]

    pl.semaphore_wait(barrier, len(peers))

    pending = []
    gu = copies(ut.at[yl], ut.at[yl], gu_s, gu_r, lpeers)
    fwd, bwd = (x + 1) % X, (x + X - 1) % X
    opp = (x + 2) % X
    nxt, prv, other = dev(fwd, y, c, z), dev(bwd, y, c, z), dev(x, y, 1 - c, z)

    def items(x_, part=None):
        r = pl.ds(0, 64) if part is None else pl.ds(32 * part, 32)
        return iaug.at[x_ * C + c, r, :]

    def gsend(x_, part, k, target):
        q = send(items(x_, part), items(x_, part), gi_s.at[k], gi_r.at[k], target)
        pending.append(q)
        return q

    far = dev(opp, y, c, z)
    fo = gsend(x, None, 3, far)
    f0 = gsend(x, None, 0, nxt)
    b0 = gsend(x, None, 1, prv)
    own = gsend(x, None, 2, other)

    lane = lax.broadcasted_iota(jnp.int32, (1, 128), 1)
    tower = lane // 16
    lane128 = lax.broadcasted_iota(jnp.int32, (128, 128), 1)
    sub16 = lax.broadcasted_iota(jnp.int32, (16, 128), 0)
    sub64 = lax.broadcasted_iota(jnp.int32, (64, 128), 0)

    def by_tower(vals, rest):
        out = jnp.full((1, 128), rest, F32)
        for k in range(4):
            out = jnp.where(tower == k, vals[k], out)
        return out

    for q in local[2:]:
        q.wait()
    owv = by_tower([ow_ref[k] for k in range(4)], 1.0)
    otv = by_tower([ot_ref[k] for k in range(4)], 0.0)
    mu = by_tower([od_ref[k] for k in range(4)], 0.0)

    def put_lambda():
        lv = lam[...]
        hi = lv.astype(BF16).astype(F32)
        r1 = lv - hi
        mid = r1.astype(BF16).astype(F32)
        lo = (r1 - mid).astype(BF16).astype(F32)
        for r in range(4 * XC):
            t = jnp.where(
                sub16 == 0, hi[r:r + 1, :],
                jnp.where(sub16 == 1, mid[r:r + 1, :],
                          jnp.where(sub16 == 2, lo[r:r + 1, :],
                                    jnp.where(sub16 == 3, 1.0, 0.0))))
            iaug[r // 4, 64:80, (r % 4) * 128:(r % 4 + 1) * 128] = t.astype(BF16)

    put_lambda()
    minus = jnp.where(sub64 < 3, -1.0, 0.0)

    def put_raw(b):
        for h in range(2):
            blk = ut[b, :, h * 128:(h + 1) * 128].astype(F32)
            rows = pl.ds(pl.multiple_of(b * 256 + h * 128, 128), 128)
            uraw[rows, :] = jnp.concatenate([blk, minus], axis=0).T.astype(BF16)

    put_raw(yl)

    b0.wait_recv()
    cf = gsend(fwd, None, 8, other)

    def put_users(muv):
        coef = owv + muv
        coef = jnp.where(lane < 64, coef, 1.0)
        for r in range(0, NU, 128):
            rows = slice(r, r + 128)
            sc = (uraw[rows, :].astype(F32) * coef).astype(BF16).astype(F32) * (1.0 / TAU)
            uaug[rows, :] = sc.astype(BF16)

    def logits(b, first):
        zt = jnp.dot(uaug[...], iaug[b], preferred_element_type=F32)
        zbuf[b] = zt
        m = jnp.maximum(jnp.maximum(zt[:, 0:128], zt[:, 128:256]),
                        jnp.maximum(zt[:, 256:384], zt[:, 384:512]))
        macc[...] = m if first else jnp.maximum(macc[...], m)

    def pass1_step(b, carry):
        logits(b, False)
        return carry

    def pass2_step(b, carry):
        mb = macc[...]
        parts = [jnp.exp(zbuf[b, :, k * 128:(k + 1) * 128] - mb) for k in range(4)]
        e16 = jnp.concatenate(parts, axis=1).astype(BF16)
        ebuf[b] = e16
        tacc[...] += lax.dot_general(
            e16, iaug[b], (((1,), (1,)), ((), ())), preferred_element_type=F32)
        return carry

    def put_numerators(q, pt):
        uf = ut[q // 2, :, (q % 2) * 128:(q % 2 + 1) * 128].astype(F32)
        prod = uf * pt
        for k in range(4):
            st[2 + k, q:q + 1, :] = jnp.sum(prod[16 * k:16 * k + 16, :], axis=0, keepdims=True)

    def lse(v):
        top = jnp.max(v, axis=0)
        return top + jnp.log(jnp.sum(jnp.exp(v - top[None]), axis=0))

    for it in range(ITERS):
        if it == 0:
            for q in gu:
                q.wait_recv()
            for d in range(1, YL):
                put_raw((yl + d) % YL)
            put_users(mu)
            logits(x * C + c, True)
            fo.wait_recv()
            co = gsend(opp, None, 9, other)
            own.wait_recv()
            logits(x * C + 1 - c, False)
            f0.wait_recv()
            cb = gsend(bwd, None, 7, other)
            logits(fwd * C + c, False)
            cf.wait_recv()
            logits(fwd * C + 1 - c, False)
            logits(opp * C + c, False)
            logits(bwd * C + c, False)
            co.wait_recv()
            logits(opp * C + 1 - c, False)
            cb.wait_recv()
            logits(bwd * C + 1 - c, False)
            pending += gu
        else:
            logits(0, True)
            lax.fori_loop(1, XC, pass1_step, 0, unroll=True)
        for q in range(NC):
            rows = slice(q * 128, (q + 1) * 128)
            m = jnp.max(macc[rows, :], axis=1, keepdims=True)
            macc[rows, :] = jnp.broadcast_to(m, (128, 128))
        last = it == ITERS - 1
        tacc[...] = jnp.zeros((NU, 128), F32)

        lax.fori_loop(0, XC, pass2_step, 0, unroll=4)

        for q in range(NC):
            rows = slice(q * 128, (q + 1) * 128)
            pt = jnp.where(lane128 == 64, macc[rows, :], tacc[rows, :]).T
            st[1, q:q + 1, :] = pt[67:68, :]
            ptn[q] = pt[0:64, :]
            st[0, q:q + 1, :] = pt[64:65, :]

        m_loc = st[0]
        s_loc = st[1]
        yll[it, y] = m_loc + jnp.log(s_loc)
        cy_l = copies(yll.at[it, y], yll.at[it, y], yl_s.at[it], yl_r.at[it], ypeers)
        for q in range(NC):
            put_numerators(q, ptn[q])
        inv = 1.0 / s_loc
        for k in range(4):
            yn[it, y, k] = st[2 + k] * inv
        cy_n = copies(yn.at[it, y], yn.at[it, y], yn_s.at[it], yn_r.at[it], ypeers)
        for q in cy_l:
            q.wait_recv()
        lv = yll[it]
        ly = lse(lv)
        zll[it, z] = ly
        cz_l = copies(zll.at[it, z], zll.at[it, z], zl_s.at[it], zl_r.at[it], zpeers)
        fy = jnp.exp(lv - ly[None])
        for q in cy_n:
            q.wait_recv()
        nv = yn[it]
        for k in range(4):
            zn[it, z, k] = jnp.sum(nv[:, k] * fy, axis=0)
        cz_n = copies(zn.at[it, z], zn.at[it, z], zn_s.at[it], zn_r.at[it], zpeers)
        for q in cz_l:
            q.wait_recv()
        lv = zll[it]
        lg = lse(lv)
        w = jnp.exp(m_loc - lg)
        if last:
            macc[0:NC, :] = TAU * lg
            out[rows_out:rows_out + 2, :] = macc[pl.ds(yl * 2, 2), :]
        whi = w.astype(BF16).astype(F32)
        r1 = w - whi
        wmid = r1.astype(BF16).astype(F32)
        wlo = (r1 - wmid).astype(BF16).astype(F32)
        for q in range(NC):
            t = jnp.where(
                sub16 == 0, whi[q:q + 1, :],
                jnp.where(sub16 == 1, wmid[q:q + 1, :],
                          jnp.where(sub16 == 2, wlo[q:q + 1, :], 0.0)))
            wl[:, q * 128:(q + 1) * 128] = t.astype(BF16)
        for b in range(XC):
            acc = jnp.dot(wl[...], ebuf[b], preferred_element_type=F32)
            row = acc[0:1, :] + acc[1:2, :] + acc[2:3, :]
            for k in range(4):
                xload[it, xc, 4 * b + k:4 * b + k + 1, :] = row[:, k * 128:(k + 1) * 128]
        cx_l = copies(xload.at[it, xc], xload.at[it, xc], xl_s.at[it], xl_r.at[it], xpeers)
        fz = jnp.exp(lv - lg[None])

        def loads_in():
            for q in cx_l:
                q.wait_recv()
            load = jnp.sum(xload[it], axis=0)
            lam[...] = jnp.maximum(
                0.0, lam[...] + DUAL_STEP * (load * (items_total / users_total) - capl[...]))

        if last:
            loads_in()
            agbuf[yl] = lam[...]
            ca = copies(agbuf.at[yl], agbuf.at[yl], ag_s, ag_r, lpeers)
        for q in cz_n:
            q.wait_recv()
        nv = zn[it]
        xach[it, xc] = jnp.zeros((8, 128), F32)
        for k in range(4):
            t = jnp.sum(nv[:, k] * fz, axis=0)
            xach[it, xc, k:k + 1, :] = jnp.sum(t, axis=0, keepdims=True)
        cx_a = copies(xach.at[it, xc], xach.at[it, xc], xa_s.at[it], xa_r.at[it], xpeers)
        if not last:
            loads_in()
            put_lambda()
        for q in cx_a:
            q.wait_recv()
        ach = jnp.sum(jnp.sum(xach[it], axis=0), axis=1, keepdims=True) / users_total
        achv = by_tower([ach[k:k + 1, :] for k in range(4)], 0.0)
        mu = mu + TARGET_STEP * (otv - achv)
        if not last:
            put_users(mu)
        pending += cy_l + cy_n + cz_l + cz_n + cx_l + cx_a

    out[rows_out + 2:rows_out + 3, :] = mu
    for q in ca:
        q.wait_recv()
    for l in range(YL):
        for xx in range(X):
            out[(xx * YL + l) * RX:(xx * YL + l + 1) * RX, :] = agbuf[l, xx * RX:(xx + 1) * RX, :]
    for q in pending + ca:
        q.wait_send()


def split_out(rows, packed, soft_out, cap_out, obj_out):
    cap_out[...] = packed[0:rows, :]
    soft_out[...] = packed[rows:rows + 2, :]
    lane = lax.broadcasted_iota(jnp.int32, (1, 128), 1)
    mu = packed[rows + 2:rows + 3, :]
    for k in range(4):
        obj_out[k] = jnp.max(jnp.where(lane == 16 * k, mu, -3.0e38))


def per_device(g, user_emb, item_emb, ow, ot, od, duals, cap):
    X, YL, C, YH, Z = g.X, g.YL, g.C, g.YH, g.Z
    Y, XC, NU = YL * YH, X * C, UD * YL
    NC = NU // 128
    rows = IB * X * YL * C // 128
    vm = pl.BlockSpec(memory_space=pltpu.VMEM)
    sm = pl.BlockSpec(memory_space=pltpu.SMEM)
    hbm = pl.BlockSpec(memory_space=pl.ANY)
    dma = pltpu.SemaphoreType.DMA
    V = pltpu.VMEM
    nl = max(YL - 1, 1)
    packed = pl.pallas_call(
        functools.partial(kernel, g),
        out_shape=jax.ShapeDtypeStruct((rows + 8, 128), F32),
        in_specs=[hbm] * 7,
        out_specs=vm,
        scratch_shapes=[
            pltpu.SMEM((4,), F32), pltpu.SMEM((4,), F32), pltpu.SMEM((4,), F32),
            V((YL, 64, UD), BF16),
            V((NU, KD), BF16),
            V((XC, KD, IB), BF16),
            V((NU, KD), BF16),
            V((XC, NU, IB), F32),
            V((XC, NU, IB), BF16),
            V((NU, 128), F32),
            V((NU, 128), F32),
            V((NC, 64, 128), F32),
            V((6, NC, 128), F32),
            V((16, NU), BF16),
            V((4 * XC, 128), F32),
            V((4 * XC, 128), F32),
            V((ITERS, Y, NC, 128), F32),
            V((ITERS, Y, 4, NC, 128), F32),
            V((ITERS, Z, NC, 128), F32),
            V((ITERS, Z, 4, NC, 128), F32),
            V((ITERS, XC, 4 * XC, 128), F32),
            V((ITERS, XC, 8, 128), F32),
            V((YL, 4 * XC, 128), F32),
            dma((5 + 2 * X,)),
            dma((10,)), dma((10,)), dma((nl,)), dma((nl,)),
            dma((ITERS, Y - 1)), dma((ITERS, Y - 1)), dma((ITERS, Y - 1)), dma((ITERS, Y - 1)),
            dma((ITERS, Z - 1)), dma((ITERS, Z - 1)), dma((ITERS, Z - 1)), dma((ITERS, Z - 1)),
            dma((ITERS, XC - 1)), dma((ITERS, XC - 1)), dma((ITERS, XC - 1)), dma((ITERS, XC - 1)),
            dma((nl,)), dma((nl,)),
        ],
        compiler_params=pltpu.CompilerParams(
            collective_id=0, has_side_effects=True, vmem_limit_bytes=60 * 1024 * 1024),
        name="dual_ascent",
    )(user_emb.T, item_emb, duals.reshape(rows, 128), cap.reshape(rows, 128), ow, ot, od)
    soft, capo, obj = pl.pallas_call(
        functools.partial(split_out, rows),
        out_shape=(
            jax.ShapeDtypeStruct((UD // 128, 128), F32),
            jax.ShapeDtypeStruct((rows, 128), F32),
            jax.ShapeDtypeStruct((4,), F32),
        ),
        in_specs=[vm],
        out_specs=(vm, vm, sm),
        name="split_out",
    )(packed)
    return soft.reshape(UD), capo.reshape(rows * 128), obj


def solution(mesh, g=SLICE):
    in_specs = (P("user", None), P(None, ("item", "user")), P(), P(), P(), P("item"), P("item"))
    out_specs = (P("user"), P("item"), P())
    return jax.shard_map(
        functools.partial(per_device, g), mesh=mesh, in_specs=in_specs, out_specs=out_specs,
        check_vma=False,
    )
```
